128 devices in a mesh: leaf: 64 (over z, y, x), rhs: 2 (over core).
Axes of the slice: x: 4, y: 4, z: 4, core: 2. Of those that a mesh axis runs over, the one named last changes fastest.
Arguments:
- rhs_block: bfloat16 [128, 524288], P('rhs', 'leaf'), may hold values from -6 to 6
- basis_t: bfloat16 [2048, 64, 256], P('leaf'), may hold values from -0.375 to 0.375
- near_blocks: bfloat16 [2048, 5, 256, 256], P('leaf'), may hold values from -0.15625 to 0.15625
- near_list: int32 [2048, 5], P('leaf'), may hold values from 0 to 2047, as said below
- leaf_transfer: bfloat16 [2048, 64, 64], P('leaf'), may hold values from -0.25 to 0.25
- couple_list: int32 [2048, 4], P('leaf'), may hold values from 0 to 2047, as said below
- leaf_couple: bfloat16 [2048, 4, 64, 64], P('leaf'), may hold values from -0.375 to 0.375
- top_transfer: bfloat16 [126, 64, 64], replicated, may hold values from -0.625 to 0.625
- top_couple: bfloat16 [126, 64, 64], replicated, may hold values from -0.75 to 0.75
Outputs:
- first_image: bfloat16 [128, 524288], P('rhs', 'leaf')
- second_image: bfloat16 [128, 524288], P('rhs', 'leaf')
The draws below stay inside these ranges and needn't reach their ends.
Inputs may be any that keep to these rules, and one draw needn't show every extreme that they name: near_list[l, 0] = l; the other entries of a row are distinct leaves at distances 1 to 16 from l, and one of them at distance exactly 16. `couple_list`: the entries of a row are distinct leaves at distances 16 + 1 to 32 from l, one of them at distance exactly 32.
All inputs are finite; a program needn't handle non-finite values.
Results may differ from the reference program's by a relative error of at most 0.0058.
Values may be sent and summed in bfloat16 or wider, within the bound.
No kernel may reach another device: no remote copies, remote signals or barrier semaphores. Data moves between devices by JAX's collectives and lax.ppermute only.
A program may use at most 128 MiB of HBM per device.

```python
import jax
import jax.numpy as jnp
from jax import lax

LEAF = 256
RANK = 64
RHS = 128
LD = 32
KN = 5
KC = 4
REACH = 16
FARR = 32
NLEAVES = 2048
NPTS = 524288
TOPN = 126
N_LEAF = 64


def partner_leaves(key, lowest, highest, wanted):
    extent = highest - lowest + 1
    scores = jax.random.randint(key, (NLEAVES, extent), 0, 1 << 20) * extent + jnp.arange(extent, dtype=jnp.int32)[None, :]
    scores = scores.at[:, extent - 1].set(-1)
    ranking = jnp.argsort(scores, axis=1)[:, :wanted]
    magnitude = (lowest + ranking).astype(jnp.int32)
    direction = jax.random.randint(jax.random.fold_in(key, 1), (NLEAVES, wanted), 0, 2) * 2 - 1
    leaf_ids = jnp.arange(NLEAVES, dtype=jnp.int32)[:, None]
    forward = leaf_ids + direction * magnitude
    outside = (forward < 0) | (forward >= NLEAVES)
    return jnp.where(outside, leaf_ids - direction * magnitude, forward).astype(jnp.int32)


def draw_near_list(key, part):
    leaf_ids = jnp.arange(NLEAVES, dtype=jnp.int32)[:, None]
    others = partner_leaves(jax.random.fold_in(key, 11), 1, REACH, KN - 1)
    return jnp.concatenate([leaf_ids, others], axis=1).astype(jnp.int32)


def draw_couple_list(key, part):
    return partner_leaves(jax.random.fold_in(key, 23), REACH + 1, FARR, KC)


def steps_of(key, shape, shards, low, largest):
    level = 1.0
    for dim, parts in shards:
        steps = jax.random.uniform(jax.random.fold_in(jax.random.fold_in(key, 6), dim), (parts,), jnp.float32, low / len(shards), largest / len(shards))
        level = level * jnp.repeat(jnp.exp(steps), shape[dim] // parts).reshape((-1,) + (1,) * (len(shape) - 1 - dim))
    return level


def noise(key, dims, deviation, most, shards=(), held_as=jnp.bfloat16):
    factor_of = steps_of(key, dims, shards, -0.22, 0.18) if shards else 1.0
    values = jax.random.normal(key, dims, jnp.float32) * deviation * factor_of
    return jnp.minimum(jnp.maximum(values, -most), most).astype(held_as)


def setup_inputs(seed: int = 0) -> dict:
    key_of = jax.random.split(jax.random.key(seed), 10)
    rhs_block = noise(key_of[0], (RHS, NPTS), 1.0, 6.0, ((0, 2), (1, 64)))
    basis_t = noise(key_of[1], (NLEAVES, RANK, LEAF), LEAF ** -0.5, 0.375, ((0, 64),))
    near_blocks = noise(key_of[2], (NLEAVES, KN, LEAF, LEAF), (LEAF * KN) ** -0.5, 0.15625, ((0, 64),))
    near_list = draw_near_list(jax.random.fold_in(key_of[9], 71), 0)
    leaf_transfer = noise(key_of[4], (NLEAVES, RANK, RANK), (RANK * LD // 4) ** -0.5, 0.25, ((0, 64),))
    couple_list = draw_couple_list(jax.random.fold_in(key_of[9], 71), 0)
    leaf_couple = noise(key_of[6], (NLEAVES, KC, RANK, RANK), (RANK * KC) ** -0.5, 0.375, ((0, 64),))
    top_transfer = noise(key_of[7], (TOPN, RANK, RANK), (3 * RANK // 2) ** -0.5, 0.625)
    top_couple = noise(key_of[8], (TOPN, RANK, RANK), RANK ** -0.5, 0.75)
    return dict(rhs_block=rhs_block, basis_t=basis_t, near_blocks=near_blocks, near_list=near_list, leaf_transfer=leaf_transfer, couple_list=couple_list, leaf_couple=leaf_couple, top_transfer=top_transfer, top_couple=top_couple)


def apply_once(vectors, basis_t, near_blocks, near_list, leaf_transfer, couple_list, leaf_couple, top_transfer, top_couple):
    levels = N_LEAF.bit_length() - 1
    hp = lax.Precision.HIGHEST
    grid = vectors.reshape(RHS, NLEAVES, LEAF)

    def group_rows(inputs):
        blocks_here, list_here = inputs
        picked = jnp.take(grid, list_here.reshape(-1).astype(jnp.int32), axis=1).reshape(RHS, LD, KN, LEAF)
        return jnp.einsum("lspr,qlsr->qlp", blocks_here.astype(jnp.float32), picked.astype(jnp.float32))

    near_groups = lax.map(group_rows, (near_blocks.reshape(N_LEAF, LD, KN, LEAF, LEAF), near_list.reshape(N_LEAF, LD, KN)))
    near_part = jnp.transpose(near_groups, (1, 0, 2, 3)).reshape(RHS, NLEAVES, LEAF)
    coefficients = jnp.einsum("lkp,qlp->lkq", basis_t.astype(jnp.float32), grid.astype(jnp.float32)).astype(jnp.bfloat16)
    partners = coefficients[couple_list.astype(jnp.int32)]
    coupled = jnp.einsum("lskm,lsmq->lkq", leaf_couple.astype(jnp.float32), partners.astype(jnp.float32))
    node_table = jnp.einsum("nlkm,nlkq->nmq", leaf_transfer.reshape(N_LEAF, LD, RANK, RANK).astype(jnp.float32), coefficients.reshape(N_LEAF, LD, RANK, RHS).astype(jnp.float32), precision=hp)
    couplings = []
    for height in range(levels):
        nodes = N_LEAF >> height
        offset = 2 * N_LEAF - 2 * nodes
        trans_here = top_transfer[offset:offset + nodes].astype(jnp.float32)
        couple_here = top_couple[offset:offset + nodes].astype(jnp.float32)
        sibling = node_table.reshape(nodes // 2, 2, RANK, RHS)[:, ::-1].reshape(nodes, RANK, RHS)
        couplings.append(jnp.einsum("nkm,nmq->nkq", couple_here, sibling, precision=hp))
        moved = jnp.einsum("nkm,nkq->nmq", trans_here, node_table, precision=hp)
        node_table = moved.reshape(nodes // 2, 2, RANK, RHS).sum(axis=1)
    descent = jnp.zeros((1, RANK, RHS), jnp.float32)
    for height in reversed(range(levels)):
        nodes = N_LEAF >> height
        offset = 2 * N_LEAF - 2 * nodes
        trans_here = top_transfer[offset:offset + nodes].astype(jnp.float32)
        parent = jnp.repeat(descent, 2, axis=0)
        descent = couplings[height] + jnp.einsum("nkm,nmq->nkq", trans_here, parent, precision=hp)
    descent_leaves = jnp.repeat(descent, LD, axis=0)
    local_far = coupled + jnp.einsum("lkm,lmq->lkq", leaf_transfer.astype(jnp.float32), descent_leaves, precision=hp)
    local_far = local_far.astype(jnp.bfloat16)
    far_part = jnp.einsum("lkp,lkq->qlp", basis_t.astype(jnp.float32), local_far.astype(jnp.float32))
    return (near_part + far_part).reshape(RHS, NPTS).astype(jnp.bfloat16)


def reference(rhs_block, basis_t, near_blocks, near_list, leaf_transfer, couple_list, leaf_couple, top_transfer, top_couple):
    first_image = apply_once(rhs_block, basis_t, near_blocks, near_list, leaf_transfer, couple_list, leaf_couple, top_transfer, top_couple)
    second_image = apply_once(first_image, basis_t, near_blocks, near_list, leaf_transfer, couple_list, leaf_couple, top_transfer, top_couple)
    return first_image, second_image
```

```python
import jax
import jax.numpy as jnp
from jax import lax
from jax.experimental import pallas as pl
from jax.experimental.pallas import tpu as pltpu
from jax.sharding import PartitionSpec as P

REACH = 16
FARR = 32
BF = jnp.bfloat16
F32 = jnp.float32
NT = (((1,), (1,)), ((), ()))
NN = (((1,), (0,)), ((), ()))


def mm(a, b, dims=NN):
    return lax.dot_general(a, b, dims, preferred_element_type=F32)


def exact(a, b, dims=NN):
    return lax.dot_general(
        a, b, dims, precision=lax.Precision.HIGHEST, preferred_element_type=F32
    )


def params(mib, *semantics):
    return pltpu.CompilerParams(
        vmem_limit_bytes=mib * 2**20, dimension_semantics=semantics or None
    )


def head_body(v, basis, trans, left, right, coef, node, acc):
    step = pl.program_id(0)
    steps = pl.num_programs(0)
    points = basis.shape[2]

    @pl.when(step == 0)
    def _():
        acc[...] = jnp.zeros_like(acc)

    @pl.when(step < steps // 2)
    def _():
        left[...] = v[...]

    @pl.when(step >= steps // 2)
    def _():
        right[...] = v[...]

    total = acc[...]
    for pair in range(basis.shape[0] // 2):
        parts = [
            mm(v[:, leaf * points : (leaf + 1) * points], basis[leaf], NT)
            for leaf in (2 * pair, 2 * pair + 1)
        ]
        both = jnp.concatenate(parts, axis=1).astype(BF)
        width = both.shape[1]
        coef[:, pair * width : (pair + 1) * width] = both
        total += mm(both, trans[pair * width : (pair + 1) * width, :])
    acc[...] = total
    node[...] = total


def head(vectors, basis_t, trans2):
    columns, own = vectors.shape
    leaves, rank, points = basis_t.shape
    steps = 4
    wide = own // steps
    some = leaves // steps
    half = steps // 2
    return pl.pallas_call(
        head_body,
        grid=(steps,),
        in_specs=[
            pl.BlockSpec((columns, wide), lambda i: (0, i)),
            pl.BlockSpec((some, rank, points), lambda i: (i, 0, 0)),
            pl.BlockSpec((some * rank, rank), lambda i: (i, 0)),
        ],
        out_specs=[
            pl.BlockSpec((columns, wide), lambda i: (0, jnp.minimum(i, half - 1))),
            pl.BlockSpec((columns, wide), lambda i: (0, jnp.maximum(i - half, 0))),
            pl.BlockSpec((columns, some * rank), lambda i: (0, i)),
            pl.BlockSpec((columns, rank), lambda i: (0, 0)),
        ],
        out_shape=[
            jax.ShapeDtypeStruct((columns, own // 2), BF),
            jax.ShapeDtypeStruct((columns, own // 2), BF),
            jax.ShapeDtypeStruct((columns, leaves * rank), BF),
            jax.ShapeDtypeStruct((columns, rank), F32),
        ],
        scratch_shapes=[pltpu.VMEM((columns, rank), F32)],
        compiler_params=params(60, "arbitrary"),
        cost_estimate=pl.CostEstimate(
            flops=200_000_000, bytes_accessed=6_000_000, transcendentals=0
        ),
        name="head",
    )(vectors, basis_t, trans2)


def table_body(levels, trans, couple, up, down, own, pair, sems):
    device = lax.axis_index("leaf")
    copies = []
    for t in range(levels):
        offset = 2 * (1 << levels) - 2 * ((1 << levels) >> t)
        here = offset + (device >> t)
        there = offset + ((device >> t) ^ 1)
        copies.append(pltpu.make_async_copy(trans.at[here], own.at[t, 0], sems.at[3 * t]))
        copies.append(pltpu.make_async_copy(trans.at[there], own.at[t, 1], sems.at[3 * t + 1]))
        copies.append(pltpu.make_async_copy(couple.at[here], pair.at[t], sems.at[3 * t + 2]))
    for copy in copies:
        copy.start()
    for copy in copies:
        copy.wait()
    up[...] = own[...].astype(F32)
    down[0] = pair[0].astype(F32)
    path = own[0, 0].astype(F32)
    for t in range(1, levels):
        down[t] = exact(path, pair[t].astype(F32))
        if t + 1 < levels:
            path = exact(path, own[t, 0].astype(F32))


def table(top_transfer, top_couple):
    rank = top_transfer.shape[1]
    devices = lax.axis_size("leaf")
    levels = devices.bit_length() - 1
    return pl.pallas_call(
        lambda *refs: table_body(levels, *refs),
        in_specs=[pl.BlockSpec(memory_space=pl.ANY)] * 2,
        out_specs=[pl.BlockSpec(memory_space=pltpu.VMEM)] * 2,
        out_shape=[
            jax.ShapeDtypeStruct((levels, 2, rank, rank), F32),
            jax.ShapeDtypeStruct((levels, rank, rank), F32),
        ],
        scratch_shapes=[
            pltpu.VMEM((levels, 2, rank, rank), BF),
            pltpu.VMEM((levels, rank, rank), BF),
            pltpu.SemaphoreType.DMA((3 * levels,)),
        ],
        compiler_params=params(60),
        cost_estimate=pl.CostEstimate(
            flops=10_000_000, bytes_accessed=3_000_000, transcendentals=0
        ),
        name="table",
    )(top_transfer, top_couple)


def tail_body(more, *refs):
    (near_list, couple_list, own_l, own_r, halo_l, halo_r, coef_own, coef_l, coef_r) = refs[:9]
    (top, near, basis, trans, couple) = refs[9:14]
    if more:
        image, left, right, coef, node = refs[14:19]
        wide, table_ref, descent, acc, sems = refs[19:]
    else:
        (image,) = refs[14:15]
        wide, table_ref, descent, sems = refs[15:]
    step = pl.program_id(0)
    steps = pl.num_programs(0)
    some = near.shape[0]
    points = basis.shape[2]
    rank = basis.shape[1]
    leaves = some * steps
    first = lax.axis_index("leaf") * leaves
    half = own_l.shape[1]

    @pl.when(step == 0)
    def _():
        copies = [
            pltpu.make_async_copy(ref, wide.at[:, i * half : (i + 1) * half], sems.at[i])
            for i, ref in enumerate((halo_l, own_l, own_r, halo_r))
        ]
        for copy in copies:
            copy.start()
        for part, ref in enumerate((coef_l, coef_own, coef_r)):
            for pair in range(leaves // 2):
                both = ref[:, 2 * rank * pair : 2 * rank * (pair + 1)]
                table_ref[part * leaves + 2 * pair] = both[:, :rank]
                table_ref[part * leaves + 2 * pair + 1] = both[:, rank:]
        high = top[...].astype(BF)
        descent[0] = high
        descent[1] = (top[...] - high.astype(F32)).astype(BF)
        if more:
            acc[...] = jnp.zeros_like(acc)
        for copy in copies:
            copy.wait()

    results = []
    for i in range(some):
        leaf = step * some + i
        moved = trans[i * rank : (i + 1) * rank, :]
        local = mm(descent[0], moved, NT) + mm(descent[1], moved, NT)
        for s in range(couple.shape[1]):
            source = couple_list[leaf, s] - first + FARR
            local += mm(table_ref[source], couple[i, s], NT)
        total = mm(local.astype(BF), basis[i])
        for s in range(near.shape[1]):
            source = near_list[leaf, s] - first + REACH
            start = pl.multiple_of(source * points, points)
            total += mm(wide[:, pl.ds(start, points)], near[i, s], NT)
        results.append(total.astype(BF))
        image[:, i * points : (i + 1) * points] = results[i]

    if more:
        @pl.when(step < steps // 2)
        def _():
            for i in range(some):
                left[:, i * points : (i + 1) * points] = results[i]

        @pl.when(step >= steps // 2)
        def _():
            for i in range(some):
                right[:, i * points : (i + 1) * points] = results[i]

        total = acc[...]
        for pair in range(some // 2):
            parts = [mm(results[i], basis[i], NT) for i in (2 * pair, 2 * pair + 1)]
            both = jnp.concatenate(parts, axis=1).astype(BF)
            width = both.shape[1]
            coef[:, pair * width : (pair + 1) * width] = both
            total += mm(both, trans[pair * width : (pair + 1) * width, :])
        acc[...] = total
        node[...] = total


def tail(more, lists, halves, halos, coefs, top, near_blocks, basis_t, trans2, leaf_couple):
    columns, half_wide = halves[0].shape
    leaves, rank, points = basis_t.shape
    kn = near_blocks.shape[1]
    kc = leaf_couple.shape[1]
    some = 2
    steps = leaves // some
    half = steps // 2
    anywhere = pl.BlockSpec(memory_space=pl.ANY)
    whole = pl.BlockSpec((columns, leaves * rank), lambda i, *_: (0, 0))
    in_specs = (
        [anywhere] * 4
        + [whole] * 3
        + [
            pl.BlockSpec((columns, rank), lambda i, *_: (0, 0)),
            pl.BlockSpec((some, kn, points, points), lambda i, *_: (i, 0, 0, 0)),
            pl.BlockSpec((some, rank, points), lambda i, *_: (i, 0, 0)),
            pl.BlockSpec((some * rank, rank), lambda i, *_: (i, 0)),
            pl.BlockSpec((some, kc, rank, rank), lambda i, *_: (i, 0, 0, 0)),
        ]
    )
    out_specs = [pl.BlockSpec((columns, some * points), lambda i, *_: (0, i))]
    out_shape = [jax.ShapeDtypeStruct((columns, leaves * points), BF)]
    scratch = [
        pltpu.VMEM((columns, 4 * half_wide), BF),
        pltpu.VMEM((3 * leaves, columns, rank), BF),
        pltpu.VMEM((2, columns, rank), BF),
    ]
    if more:
        out_specs += [
            pl.BlockSpec((columns, some * points), lambda i, *_: (0, jnp.minimum(i, half - 1))),
            pl.BlockSpec((columns, some * points), lambda i, *_: (0, jnp.maximum(i - half, 0))),
            pl.BlockSpec((columns, some * rank), lambda i, *_: (0, i)),
            pl.BlockSpec((columns, rank), lambda i, *_: (0, 0)),
        ]
        out_shape += [
            jax.ShapeDtypeStruct((columns, half_wide), BF),
            jax.ShapeDtypeStruct((columns, half_wide), BF),
            jax.ShapeDtypeStruct((columns, leaves * rank), BF),
            jax.ShapeDtypeStruct((columns, rank), F32),
        ]
        scratch.append(pltpu.VMEM((columns, rank), F32))
    scratch.append(pltpu.SemaphoreType.DMA((4,)))
    return pl.pallas_call(
        lambda *refs: tail_body(more, *refs),
        grid_spec=pltpu.PrefetchScalarGridSpec(
            num_scalar_prefetch=2,
            grid=(steps,),
            in_specs=in_specs,
            out_specs=out_specs,
            scratch_shapes=scratch,
        ),
        out_shape=out_shape,
        compiler_params=params(44, "arbitrary"),
        cost_estimate=pl.CostEstimate(
            flops=1_700_000_000, bytes_accessed=30_000_000, transcendentals=0
        ),
        name="tail",
    )(*lists, *halves, *halos, *coefs, top, near_blocks, basis_t, trans2, leaf_couple)


def from_left(value):
    ends = lax.axis_size("leaf") - 1
    return lax.ppermute(value, "leaf", [(i, i + 1) for i in range(ends)])


def from_right(value):
    ends = lax.axis_size("leaf") - 1
    return lax.ppermute(value, "leaf", [(i + 1, i) for i in range(ends)])


def swapped(value, mask):
    return lax.ppermute(value, "leaf", [(i, i ^ mask) for i in range(lax.axis_size("leaf"))])


def exchange(left, right, coef, node, up, down):
    levels = up.shape[0]
    top = jnp.zeros_like(node)
    held = None
    for t in range(levels):
        mask = (1 << t) if t % 2 == 0 else 3 << (t - 1)
        other = swapped(node, mask)
        top += exact(other, down[t], NT)
        if t == 1:
            left, right, coef, other = lax.optimization_barrier((left, right, coef, other))
            held = (from_left(right), from_right(left), from_left(coef), from_right(coef))
        if t + 1 < levels:
            node = exact(node, up[t, 0]) + exact(other, up[t, 1])
    return top, held[:2], (held[2], coef, held[3])


def on_device(
    rhs_block,
    basis_t,
    near_blocks,
    near_list,
    leaf_transfer,
    couple_list,
    leaf_couple,
    top_transfer,
    top_couple,
):
    leaves, rank, _ = leaf_transfer.shape
    trans2 = leaf_transfer.reshape(leaves * rank, rank)
    lists = (near_list, couple_list)
    fixed = (near_blocks, basis_t, trans2, leaf_couple)
    up, down = table(top_transfer, top_couple)
    left, right, coef, node = head(rhs_block, basis_t, trans2)
    top, halos, coefs = exchange(left, right, coef, node, up, down)
    first_image, left, right, coef, node = tail(
        True, lists, (left, right), halos, (coefs[1], coefs[0], coefs[2]), top, *fixed
    )
    top, halos, coefs = exchange(left, right, coef, node, up, down)
    (second_image,) = tail(
        False, lists, (left, right), halos, (coefs[1], coefs[0], coefs[2]), top, *fixed
    )
    return (first_image, second_image)


def solution(mesh):
    in_specs = (
        P("rhs", "leaf"),
        P("leaf", None, None),
        P("leaf", None, None, None),
        P("leaf", None),
        P("leaf", None, None),
        P("leaf", None),
        P("leaf", None, None, None),
        P(),
        P(),
    )
    out_specs = (P("rhs", "leaf"), P("rhs", "leaf"))
    return jax.shard_map(
        on_device, mesh=mesh, in_specs=in_specs, out_specs=out_specs, check_vma=False
    )
```

```python
import jax
import jax.numpy as jnp
from jax import lax
from jax.experimental import pallas as pl
from jax.experimental.pallas import tpu as pltpu
from jax.sharding import PartitionSpec as P


REACH = 16
FARR = 32
PIECES = 4
BF = jnp.bfloat16
F32 = jnp.float32
NT = (((1,), (1,)), ((), ()))
NN = (((1,), (0,)), ((), ()))
HBM = pl.BlockSpec(memory_space=pltpu.HBM)
VMEM = pl.BlockSpec(memory_space=pltpu.VMEM)


def mm(a, b, dims=NN):
    return lax.dot_general(a, b, dims, preferred_element_type=F32)


def exact(a, b, dims=NN):
    return lax.dot_general(
        a, b, dims, precision=lax.Precision.HIGHEST, preferred_element_type=F32
    )


def params(mib):
    return pltpu.CompilerParams(vmem_limit_bytes=mib * 2**20)


def cost(flops, moved):
    return pl.CostEstimate(flops=flops, bytes_accessed=moved, transcendentals=0)


def is_even():
    return (lax.axis_index("leaf") & 1) == 0


def columns_of(start, width):
    return pl.ds(pl.multiple_of(start, width), width)


def head_body(v, basis_hbm, trans_hbm, a, b, node, basis, trans, sems):
    leaves, rank, points = basis.shape
    half = v.shape[1] // 2
    first_a = jnp.where(is_even(), leaves // 2, 0)
    sides = ((a, first_a), (b, leaves // 2 - first_a))
    copies = [
        pltpu.make_async_copy(
            v.at[:, columns_of(first * points, half)], msg.at[:, :half], sems.at[i]
        )
        for i, (msg, first) in enumerate(sides)
    ]
    copies.append(pltpu.make_async_copy(basis_hbm, basis, sems.at[2]))
    copies.append(pltpu.make_async_copy(trans_hbm, trans, sems.at[3]))
    for i in (2, 0, 3, 1):
        copies[i].start()
    copies[2].wait()
    total = None
    for side, (msg, first) in enumerate(sides):
        copies[side].wait()
        if side == 0:
            copies[3].wait()
        for pair in range(leaves // 4):
            parts = [
                mm(msg[:, leaf * points : (leaf + 1) * points], basis[first + leaf], NT)
                for leaf in (2 * pair, 2 * pair + 1)
            ]
            both = jnp.concatenate(parts, axis=1).astype(BF)
            start = (first // 2 + pair) * 2 * rank
            a[:, columns_of(half + start, 2 * rank)] = both
            b[:, columns_of(half + start, 2 * rank)] = both
            term = mm(both, trans[columns_of(start, 2 * rank), :])
            total = term if total is None else total + term
    node[...] = total


def head(vectors, basis_t, trans2):
    columns, own = vectors.shape
    leaves, rank, _ = basis_t.shape
    message = jax.ShapeDtypeStruct((columns, own // 2 + leaves * rank), BF)
    return pl.pallas_call(
        head_body,
        in_specs=[HBM] * 3,
        out_specs=[VMEM] * 3,
        out_shape=[message, message, jax.ShapeDtypeStruct((columns, rank), F32)],
        scratch_shapes=[
            pltpu.VMEM(basis_t.shape, BF),
            pltpu.VMEM(trans2.shape, BF),
            pltpu.SemaphoreType.DMA((4,)),
        ],
        compiler_params=params(10),
        cost_estimate=cost(200_000_000, 6_000_000),
        name="head",
    )(*(pltpu.with_memory_space_constraint(x, pltpu.HBM) for x in (vectors, basis_t, trans2)))


def table_body(levels, trans, couple, up, down, own, pair):
    device = lax.axis_index("leaf")
    count, rows, nodes = 8, trans.shape[0], trans.shape[2]
    row = lax.broadcasted_iota(jnp.int32, (count, nodes), 0)
    node = lax.broadcasted_iota(jnp.int32, (count, nodes), 1)
    offset = (2 << levels) - lax.shift_right_logical(jnp.full_like(row, 2 << levels), row)
    here = offset + lax.shift_right_logical(jnp.zeros_like(row) + device, row)
    there = jnp.bitwise_xor(here, 1)
    wanted = row < levels
    pick_here = jnp.where(wanted & (node == here), 1.0, 0.0).astype(BF)
    pick_there = jnp.where(wanted & (node == there), 1.0, 0.0).astype(BF)
    both = jnp.concatenate([pick_here, pick_there], axis=0)
    for k in range(rows):
        own[:, k, :] = mm(both, trans[k], NT)
        pair[:, k, :] = mm(pick_here, couple[k], NT)
    for t in range(levels):
        up[t, 0] = own[t]
        up[t, 1] = own[count + t]
    down[0] = pair[0]
    path = own[0]
    for t in range(1, levels):
        down[t] = exact(path, pair[t])
        if t + 1 < levels:
            path = exact(path, own[t])


def table(top_transfer, top_couple):
    rank = top_transfer.shape[1]
    levels = lax.axis_size("leaf").bit_length() - 1
    return pl.pallas_call(
        lambda *refs: table_body(levels, *refs),
        in_specs=[VMEM] * 2,
        out_specs=[VMEM] * 2,
        out_shape=[
            jax.ShapeDtypeStruct((levels, 2, rank, rank), F32),
            jax.ShapeDtypeStruct((levels, rank, rank), F32),
        ],
        scratch_shapes=[pltpu.VMEM((16, rank, rank), F32), pltpu.VMEM((8, rank, rank), F32)],
        compiler_params=params(10),
        cost_estimate=cost(10_000_000, 3_000_000),
        name="table",
    )(jnp.transpose(top_transfer, (1, 2, 0)), jnp.transpose(top_couple, (1, 2, 0)))


def near_body(piece, load, near_list, v, near, *refs):
    if load:
        total, kept, sems = refs
    else:
        (total,) = refs
        kept = near
    some, kn, points, _ = kept.shape
    leaves = v.shape[1] // points
    first = lax.axis_index("leaf") * leaves
    group = 4
    copies = []
    if load:
        for g in range(some // group):
            here = pl.ds(piece * some + g * group, group)
            copies.append(
                pltpu.make_async_copy(near.at[here], kept.at[pl.ds(g * group, group)], sems.at[g])
            )
            copies[-1].start()
    for i in range(some):
        if load and i % group == 0:
            copies[i // group].wait()
        out = None
        for s in range(kn):
            source = near_list[piece * some + i, s] - first
            inside = (source >= 0) & (source < leaves)
            rows = v[:, columns_of(jnp.clip(source, 0, leaves - 1) * points, points)]
            term = mm(jnp.where(inside, rows, jnp.zeros_like(rows)), kept[i, s], NT)
            out = term if out is None else out + term
        total[:, i * points : (i + 1) * points] = out


def near_piece(piece, near_list, v, near_blocks, kept):
    columns = v.shape[0]
    load = kept is None
    shape = near_blocks.shape
    some = shape[0] // PIECES
    out_shape = [jax.ShapeDtypeStruct((columns, some * shape[2]), F32)]
    scratch = []
    if load:
        out_shape.append(jax.ShapeDtypeStruct((some, *shape[1:]), BF))
        scratch.append(pltpu.SemaphoreType.DMA((some // 4,)))
    out = pl.pallas_call(
        lambda *refs: near_body(piece, load, *refs),
        grid_spec=pltpu.PrefetchScalarGridSpec(
            num_scalar_prefetch=1,
            in_specs=[VMEM, HBM if load else VMEM],
            out_specs=[VMEM] * len(out_shape),
            scratch_shapes=scratch,
        ),
        out_shape=out_shape,
        compiler_params=params(10),
        cost_estimate=cost(350_000_000, 6_000_000),
    )(near_list, v, pltpu.with_memory_space_constraint(near_blocks, pltpu.HBM) if load else kept)
    return out[0], (out[1] if load else kept)


def halo_plan(near_list):
    leaves, kn = near_list.shape
    first = lax.axis_index("leaf") * leaves
    source = [near_list[:, s] - first for s in range(kn)]
    outside = [(j < 0) | (j >= leaves) for j in source]
    code = [
        jnp.where(j < 0, j + REACH, j - leaves + REACH) + 64 * s for s, j in enumerate(source)
    ]
    place = []
    count = jnp.zeros_like(source[0])
    for out in outside:
        place.append(count)
        count = count + out.astype(jnp.int32)
    rows = []
    for j in range(kn - 1):
        row = jnp.full_like(count, -1)
        for s in range(kn):
            row = jnp.where(outside[s] & (place[s] == j), code[s], row)
        rows.append(row)
    most = jnp.max(count.reshape(PIECES, -1), axis=1)
    rows.append(jnp.pad(most, (0, leaves - PIECES)))
    return jnp.stack(rows)


def tail_body(more, plan, couple_list, got_a, got_b, sent_a, top, basis, trans, couple, *refs):
    kept, partial, refs = refs[:PIECES], refs[PIECES : 2 * PIECES], refs[2 * PIECES :]
    if more:
        image, a, b, node, table_ref, acc, total_ref = refs
    else:
        image, table_ref, acc, staged, sems = refs
    leaves, rank, points = basis.shape
    some = leaves // PIECES
    half = leaves // 2 * points
    even = is_even()
    first = lax.axis_index("leaf") * leaves
    base_a = jnp.where(even, 2 * leaves, 0)
    for ref, base in ((got_a, base_a), (sent_a, leaves), (got_b, 2 * leaves - base_a)):
        for pair in range(leaves // 2):
            start = half + 2 * rank * pair
            both = ref[:, start : start + 2 * rank]
            table_ref[base + 2 * pair] = both[:, :rank]
            table_ref[base + 2 * pair + 1] = both[:, rank:]
    high = top[...].astype(BF)
    low = (top[...] - high.astype(F32)).astype(BF)
    if more:
        total_ref[...] = jnp.zeros_like(total_ref)
    writes = []
    for piece in range(PIECES):
        near, own = kept[piece], partial[piece]
        acc[...] = own[...]

        def add(j, carry, near=near, piece=piece):
            for i in range(some):
                code = plan[j, piece * some + i]
                there = code >= 0
                code = jnp.maximum(code, 0)
                place = code & 31
                at = columns_of((place & 15) * points, points)
                in_a = (place >= REACH) == even
                rows = jnp.where(in_a, got_a[:, at], got_b[:, at])
                rows = jnp.where(there, rows, jnp.zeros_like(rows))
                here = slice(i * points, (i + 1) * points)
                acc[:, here] += mm(rows, near[i, lax.shift_right_logical(code, 6)], NT)
            return carry

        lax.fori_loop(0, plan[4, piece], add, 0)
        results = []
        for i in range(some):
            leaf = piece * some + i
            moved = trans[leaf * rank : (leaf + 1) * rank, :]
            local = mm(high, moved, NT) + mm(low, moved, NT)
            for s in range(couple.shape[1]):
                local += mm(table_ref[couple_list[leaf, s] - first + FARR], couple[leaf, s], NT)
            here = slice(i * points, (i + 1) * points)
            value = (acc[:, here] + mm(local.astype(BF), basis[leaf])).astype(BF)
            results.append(value)
            if more:
                image[:, leaf * points : (leaf + 1) * points] = value
            else:
                staged[:, leaf * points : (leaf + 1) * points] = value
        if not more:
            here = pl.ds(piece * some * points, some * points)
            writes.append(pltpu.make_async_copy(staged.at[:, here], image.at[:, here], sems.at[piece]))
            writes[-1].start()
            continue
        for pair in range(some // 2):
            leaf = piece * some + 2 * pair
            parts = [mm(results[2 * pair + i], basis[leaf + i], NT) for i in range(2)]
            both = jnp.concatenate(parts, axis=1).astype(BF)
            a[:, half + leaf * rank : half + (leaf + 2) * rank] = both
            b[:, half + leaf * rank : half + (leaf + 2) * rank] = both
            total_ref[...] += mm(both, trans[leaf * rank : (leaf + 2) * rank, :])
        in_right = piece >= PIECES // 2
        start = piece % (PIECES // 2) * some * points

        def put(message, results=results, start=start):
            for i, value in enumerate(results):
                message[:, start + i * points : start + (i + 1) * points] = value

        @pl.when(even == in_right)
        def _():
            put(a)

        @pl.when(even != in_right)
        def _():
            put(b)

    for write in writes:
        write.wait()
    if more:
        node[...] = total_ref[...]


def tail(more, lists, got, sent_a, top, kept, partial, basis_t, trans2, leaf_couple):
    columns, wide = sent_a.shape
    leaves, rank, points = basis_t.shape
    own = leaves * points
    image = jax.ShapeDtypeStruct((columns, own), BF)
    scratch = [
        pltpu.VMEM((3 * leaves, columns, rank), BF),
        pltpu.VMEM((columns, own // PIECES), F32),
    ]
    if more:
        message = jax.ShapeDtypeStruct((columns, wide), BF)
        out_shape = [image, message, message, jax.ShapeDtypeStruct((columns, rank), F32)]
        out_specs = [VMEM] * 4
        scratch.append(pltpu.VMEM((columns, rank), F32))
    else:
        out_shape, out_specs = [image], [HBM]
        scratch += [pltpu.VMEM((columns, own), BF), pltpu.SemaphoreType.DMA((PIECES,))]
    return pl.pallas_call(
        lambda *refs: tail_body(more, *refs),
        grid_spec=pltpu.PrefetchScalarGridSpec(
            num_scalar_prefetch=2,
            in_specs=[VMEM] * (7 + 2 * PIECES),
            out_specs=out_specs,
            scratch_shapes=scratch,
        ),
        out_shape=out_shape,
        compiler_params=params(16),
        cost_estimate=cost(1_000_000_000, 10_000_000),
        name="tail",
    )(*lists, *got, sent_a, top, basis_t, trans2, leaf_couple, *kept, *partial)


def swapped(value, mask):
    return lax.ppermute(value, "leaf", [(i, i ^ mask) for i in range(lax.axis_size("leaf"))])


def swapped_odd(value):
    size = lax.axis_size("leaf")
    pairs = [(i, i + 1) for i in range(1, size - 1, 2)]
    return lax.ppermute(value, "leaf", pairs + [(j, i) for i, j in pairs])


def one_product(more, v, a, b, node, up, down, kept, plan, near_list, couple_list, near_blocks, *fixed):
    levels = up.shape[0]
    top = jnp.zeros_like(node)
    got_a = got_b = None
    partial, held = [], []
    for t in range(levels):
        mask = (1 << t) if t % 2 == 0 else 3 << (t - 1)
        other = swapped(node, mask)
        if t >= 2:
            piece = t - 2
            own, block = near_piece(piece, near_list, v, near_blocks, kept[piece] if kept else None)
            partial.append(own)
            held.append(block)
        if t == 0:
            a, other = lax.optimization_barrier((a, other))
            got_a = swapped(a, 1)
        if t == 1:
            b, other = lax.optimization_barrier((b, other))
            got_b = swapped_odd(b)
        if t + 1 < levels:
            node = exact(node, up[t, 0]) + exact(other, up[t, 1])
        top += exact(other, down[t], NT)
    out = tail(more, (plan, couple_list), (got_a, got_b), a, top, held, partial, *fixed)
    return out, held


def on_device(
    rhs_block,
    basis_t,
    near_blocks,
    near_list,
    leaf_transfer,
    couple_list,
    leaf_couple,
    top_transfer,
    top_couple,
):
    leaves, rank, _ = leaf_transfer.shape
    trans2 = leaf_transfer.reshape(leaves * rank, rank)
    a, b, node = head(rhs_block, basis_t, trans2)
    up, down = table(top_transfer, top_couple)
    plan = halo_plan(near_list)
    lists = (plan, near_list, couple_list, near_blocks, basis_t, trans2, leaf_couple)
    (first_image, a, b, node), kept = one_product(
        True, rhs_block, a, b, node, up, down, None, *lists
    )
    (second_image,), _ = one_product(
        False, first_image, a, b, node, up, down, kept, *lists
    )
    return (first_image, second_image)


def solution(mesh):
    in_specs = (
        P("rhs", "leaf"),
        P("leaf", None, None),
        P("leaf", None, None, None),
        P("leaf", None),
        P("leaf", None, None),
        P("leaf", None),
        P("leaf", None, None, None),
        P(),
        P(),
    )
    out_specs = (P("rhs", "leaf"), P("rhs", "leaf"))
    return jax.shard_map(
        on_device, mesh=mesh, in_specs=in_specs, out_specs=out_specs, check_vma=False
    )
```

```python
import jax
import jax.numpy as jnp
from jax import lax
from jax.experimental import pallas as pl
from jax.experimental.pallas import tpu as pltpu
from jax.sharding import PartitionSpec as P


REACH = 16
FARR = 32
PIECES = 4
TOGETHER = 4
STRIDE = 40
BF = jnp.bfloat16
F32 = jnp.float32
NT = (((1,), (1,)), ((), ()))
NN = (((1,), (0,)), ((), ()))
HBM = pl.BlockSpec(memory_space=pltpu.HBM)
VMEM = pl.BlockSpec(memory_space=pltpu.VMEM)


def mm(a, b, dims=NN):
    return lax.dot_general(a, b, dims, preferred_element_type=F32)


def exact(a, b, dims=NN):
    return lax.dot_general(
        a, b, dims, precision=lax.Precision.HIGHEST, preferred_element_type=F32
    )


def params(mib):
    return pltpu.CompilerParams(vmem_limit_bytes=mib * 2**20)


def cost(flops, moved):
    return pl.CostEstimate(flops=flops, bytes_accessed=moved, transcendentals=0)


def is_even():
    return (lax.axis_index("leaf") & 1) == 0


def columns_of(start, width):
    return pl.ds(pl.multiple_of(start, width), width)


def split_body(v, va, vb, sems):
    half = va.shape[1]
    start_a = jnp.where(is_even(), half, 0)
    copies = [
        pltpu.make_async_copy(v.at[:, columns_of(start, half)], out, sems.at[i])
        for i, (out, start) in enumerate(((va, start_a), (vb, half - start_a)))
    ]
    for copy in copies:
        copy.start()
    for copy in copies:
        copy.wait()


def split(vectors):
    columns, own = vectors.shape
    return pl.pallas_call(
        split_body,
        in_specs=[HBM],
        out_specs=[VMEM] * 2,
        out_shape=[jax.ShapeDtypeStruct((columns, own // 2), BF)] * 2,
        scratch_shapes=[pltpu.SemaphoreType.DMA((2,))],
        compiler_params=params(4),
        cost_estimate=cost(0, 2_000_000),
        name="split",
    )(pltpu.with_memory_space_constraint(vectors, pltpu.HBM))


def head_body(va, vb, basis_hbm, trans_hbm, coef, node, basis, trans, sems):
    leaves, rank, points = basis.shape
    first_a = jnp.where(is_even(), leaves // 2, 0)
    copies = [
        pltpu.make_async_copy(basis_hbm, basis, sems.at[0]),
        pltpu.make_async_copy(trans_hbm, trans, sems.at[1]),
    ]
    for copy in copies:
        copy.start()
    for copy in copies:
        copy.wait()
    total = None
    for v, first in ((va, first_a), (vb, leaves // 2 - first_a)):
        for pair in range(leaves // 4):
            parts = [
                mm(v[:, leaf * points : (leaf + 1) * points], basis[first + leaf], NT)
                for leaf in (2 * pair, 2 * pair + 1)
            ]
            both = jnp.concatenate(parts, axis=1).astype(BF)
            at = columns_of((first // 2 + pair) * 2 * rank, 2 * rank)
            coef[:, at] = both
            term = mm(both, trans[at, :])
            total = term if total is None else total + term
    node[...] = total


def head(va, vb, basis_t, trans2):
    columns = va.shape[0]
    leaves, rank, _ = basis_t.shape
    hbm = (pltpu.with_memory_space_constraint(x, pltpu.HBM) for x in (basis_t, trans2))
    return pl.pallas_call(
        head_body,
        in_specs=[VMEM] * 2 + [HBM] * 2,
        out_specs=[VMEM] * 2,
        out_shape=[
            jax.ShapeDtypeStruct((columns, leaves * rank), BF),
            jax.ShapeDtypeStruct((columns, rank), F32),
        ],
        scratch_shapes=[
            pltpu.VMEM(basis_t.shape, BF),
            pltpu.VMEM(trans2.shape, BF),
            pltpu.SemaphoreType.DMA((2,)),
        ],
        compiler_params=params(6),
        cost_estimate=cost(200_000_000, 6_000_000),
        name="head",
    )(va, vb, *hbm)


def table_body(levels, near_list, trans_hbm, couple_hbm, near, up, down, plan, kept, *scratch):
    trans, couple, own, pair, sems = scratch
    copies = [
        pltpu.make_async_copy(trans_hbm, trans, sems.at[0]),
        pltpu.make_async_copy(couple_hbm, couple, sems.at[1]),
        pltpu.make_async_copy(near.at[pl.ds(0, kept.shape[0])], kept, sems.at[2]),
    ]
    for copy in copies:
        copy.start()
    device = lax.axis_index("leaf")
    kn, leaves = near_list.shape
    some = leaves // PIECES
    first = device * leaves

    for piece in range(PIECES):

        def scan(i, n, piece=piece):
            leaf = piece * some + i
            for s in range(kn):
                source = near_list[s, leaf] - first
                left = source < 0
                place = source + jnp.where(left, REACH, REACH - leaves)
                plan[piece * STRIDE + n] = (leaf * 8 + s) * 32 + place
                n = n + jnp.where(left | (source >= leaves), 1, 0)
            return n

        count = lax.fori_loop(0, some, scan, 0)
        for i in range(TOGETHER):
            plan[piece * STRIDE + count + i] = (leaves * 8) * 32
        plan[PIECES * STRIDE + piece] = lax.div(count + TOGETHER - 1, TOGETHER)

    count, rows, nodes = 8, trans.shape[0], trans.shape[2]
    row = lax.broadcasted_iota(jnp.int32, (count, nodes), 0)
    node = lax.broadcasted_iota(jnp.int32, (count, nodes), 1)
    offset = (2 << levels) - lax.shift_right_logical(jnp.full_like(row, 2 << levels), row)
    here = offset + lax.shift_right_logical(jnp.zeros_like(row) + device, row)
    there = jnp.bitwise_xor(here, 1)
    wanted = row < levels
    pick_here = jnp.where(wanted & (node == here), 1.0, 0.0).astype(BF)
    pick_there = jnp.where(wanted & (node == there), 1.0, 0.0).astype(BF)
    both = jnp.concatenate([pick_here, pick_there], axis=0)
    copies[0].wait()
    copies[1].wait()
    for k in range(rows):
        own[:, k, :] = mm(both, trans[k], NT)
        pair[:, k, :] = mm(pick_here, couple[k], NT)
    for t in range(levels):
        up[t, 0] = own[t]
        up[t, 1] = own[count + t]
    down[0] = pair[0]
    path = own[0]
    for t in range(1, levels):
        down[t] = exact(path, pair[t])
        if t + 1 < levels:
            path = exact(path, own[t])
    copies[2].wait()


def table(top_transfer, top_couple, near_list_t, near_blocks):
    nodes, rank, _ = top_transfer.shape
    levels = lax.axis_size("leaf").bit_length() - 1
    shape = near_blocks.shape
    hbm = (
        jnp.transpose(top_transfer, (1, 2, 0)),
        jnp.transpose(top_couple, (1, 2, 0)),
        near_blocks,
    )
    return pl.pallas_call(
        lambda *refs: table_body(levels, *refs),
        grid_spec=pltpu.PrefetchScalarGridSpec(
            num_scalar_prefetch=1,
            in_specs=[HBM] * 3,
            out_specs=[VMEM, VMEM, pl.BlockSpec(memory_space=pltpu.SMEM), VMEM],
            scratch_shapes=[
                pltpu.VMEM((rank, rank, nodes), BF),
                pltpu.VMEM((rank, rank, nodes), BF),
                pltpu.VMEM((16, rank, rank), F32),
                pltpu.VMEM((8, rank, rank), F32),
                pltpu.SemaphoreType.DMA((3,)),
            ],
        ),
        out_shape=[
            jax.ShapeDtypeStruct((levels, 2, rank, rank), F32),
            jax.ShapeDtypeStruct((levels, rank, rank), F32),
            jax.ShapeDtypeStruct((PIECES * STRIDE + 8,), jnp.int32),
            jax.ShapeDtypeStruct((shape[0] // PIECES, *shape[1:]), BF),
        ],
        compiler_params=params(6),
        cost_estimate=cost(10_000_000, 8_000_000),
        name="table",
    )(near_list_t, *(pltpu.with_memory_space_constraint(x, pltpu.HBM) for x in hbm))


def near_body(piece, load, near_list, v, kept, *refs):
    if load:
        near, total, later, sem = refs
        here = pl.ds((piece + 1) * later.shape[0], later.shape[0])
        copy = pltpu.make_async_copy(near.at[here], later, sem)
        copy.start()
    else:
        (total,) = refs
    some, kn, points, _ = kept.shape
    leaves = v.shape[1] // points
    first = lax.axis_index("leaf") * leaves
    for i in range(some):
        out = None
        for s in range(kn):
            source = near_list[s, piece * some + i] - first
            inside = (source >= 0) & (source < leaves)
            rows = v[:, columns_of(jnp.clip(source, 0, leaves - 1) * points, points)]
            term = mm(jnp.where(inside, rows, jnp.zeros_like(rows)), kept[i, s], NT)
            out = term if out is None else out + term
        total[:, i * points : (i + 1) * points] = out
    if load:
        copy.wait()


def near_piece(piece, near_list_t, v, near_blocks, kept, load):
    columns = v.shape[0]
    some, _, points, _ = kept.shape
    in_specs = [VMEM, VMEM]
    args = [v, kept]
    out_shape = [jax.ShapeDtypeStruct((columns, some * points), F32)]
    scratch = []
    if load:
        in_specs.append(HBM)
        args.append(pltpu.with_memory_space_constraint(near_blocks, pltpu.HBM))
        out_shape.append(jax.ShapeDtypeStruct(kept.shape, BF))
        scratch.append(pltpu.SemaphoreType.DMA)
    return pl.pallas_call(
        lambda *refs: near_body(piece, load, *refs),
        grid_spec=pltpu.PrefetchScalarGridSpec(
            num_scalar_prefetch=1,
            in_specs=in_specs,
            out_specs=[VMEM] * len(out_shape),
            scratch_shapes=scratch,
        ),
        out_shape=out_shape,
        compiler_params=params(4),
        cost_estimate=cost(350_000_000, 6_000_000),
    )(near_list_t, *args)


def tail_body(more, plan, couple_list, *refs):
    got_va, got_vb, got_ca, got_cb, sent_c, top, basis, trans, couple = refs[:9]
    refs = refs[9:]
    kept, partial, refs = refs[:PIECES], refs[PIECES : 2 * PIECES], refs[2 * PIECES :]
    if more:
        image, own_v, va, vb, coef, node, table_ref, wide, acc, total_ref, sems = refs
    else:
        image, own_v, table_ref, wide, acc, sems = refs
    leaves, rank, points = basis.shape
    some = leaves // PIECES
    half = leaves // 2 * points
    even = is_even()
    first = lax.axis_index("leaf") * leaves
    start_a = jnp.where(even, half, 0)
    copies = [
        pltpu.make_async_copy(ref, wide.at[:, columns_of(start, half)], sems.at[i])
        for i, (ref, start) in enumerate(((got_va, start_a), (got_vb, half - start_a)))
    ]
    for copy in copies:
        copy.start()
    base_a = jnp.where(even, 2 * leaves, 0)
    for ref, base in ((got_ca, base_a), (sent_c, leaves), (got_cb, 2 * leaves - base_a)):
        for pair in range(leaves // 2):
            both = ref[:, 2 * rank * pair : 2 * rank * (pair + 1)]
            table_ref[base + 2 * pair] = both[:, :rank]
            table_ref[base + 2 * pair + 1] = both[:, rank:]
    high = top[...].astype(BF)
    low = (top[...] - high.astype(F32)).astype(BF)
    if more:
        total_ref[...] = jnp.zeros_like(total_ref)
    for piece in range(PIECES):
        width = some * points
        acc[:, piece * width : (piece + 1) * width] = partial[piece][...]
    for copy in copies:
        copy.wait()
    writes = []
    for piece in range(PIECES):
        near = kept[piece]

        def add(j, carry, near=near, piece=piece):
            terms = []
            for i in range(TOGETHER):
                code = plan[piece * STRIDE + j * TOGETHER + i]
                block = lax.shift_right_logical(code, 5)
                leaf = lax.shift_right_logical(code, 8)
                rows = wide[:, columns_of((code & 31) * points, points)]
                term = mm(rows, near[leaf & (some - 1), block & 7], NT)
                terms.append((columns_of(leaf * points, points), term))
            for here, term in terms:
                acc[:, here] += term
            return carry

        lax.fori_loop(0, plan[PIECES * STRIDE + piece], add, 0)
        results = []
        for i in range(some):
            leaf = piece * some + i
            moved = trans[leaf * rank : (leaf + 1) * rank, :]
            local = mm(high, moved, NT) + mm(low, moved, NT)
            for s in range(couple.shape[1]):
                local += mm(table_ref[couple_list[s, leaf] - first + FARR], couple[leaf, s], NT)
            here = slice(leaf * points, (leaf + 1) * points)
            value = (acc[:, here] + mm(local.astype(BF), basis[leaf])).astype(BF)
            results.append(value)
            own_v[:, here] = value
        here = pl.ds(piece * some * points, some * points)
        writes.append(pltpu.make_async_copy(own_v.at[:, here], image.at[:, here], sems.at[2 + piece]))
        writes[-1].start()
        if not more:
            continue
        for pair in range(some // 2):
            leaf = piece * some + 2 * pair
            parts = [mm(results[2 * pair + i], basis[leaf + i], NT) for i in range(2)]
            both = jnp.concatenate(parts, axis=1).astype(BF)
            coef[:, leaf * rank : (leaf + 2) * rank] = both
            total_ref[...] += mm(both, trans[leaf * rank : (leaf + 2) * rank, :])
        in_right = piece >= PIECES // 2
        start = piece % (PIECES // 2) * some * points

        def put(message, results=results, start=start):
            for i, value in enumerate(results):
                message[:, start + i * points : start + (i + 1) * points] = value

        @pl.when(even == in_right)
        def _():
            put(va)

        @pl.when(even != in_right)
        def _():
            put(vb)

    if more:
        node[...] = total_ref[...]
    for write in writes:
        write.wait()


def tail(more, lists, got, sent_c, top, kept, partial, basis_t, trans2, leaf_couple):
    columns = sent_c.shape[0]
    leaves, rank, points = basis_t.shape
    own = leaves * points
    image = jax.ShapeDtypeStruct((columns, own), BF)
    out_shape, out_specs = [image], [HBM]
    scratch = [
        pltpu.VMEM((3 * leaves, columns, rank), BF),
        pltpu.VMEM((columns, own), BF),
        pltpu.VMEM((columns, own + points), F32),
    ]
    if more:
        half = jax.ShapeDtypeStruct((columns, own // 2), BF)
        out_shape += [
            image,
            half,
            half,
            jax.ShapeDtypeStruct((columns, leaves * rank), BF),
            jax.ShapeDtypeStruct((columns, rank), F32),
        ]
        out_specs += [VMEM] * 5
        scratch.append(pltpu.VMEM((columns, rank), F32))
    else:
        scratch.insert(0, pltpu.VMEM((columns, own), BF))
    scratch.append(pltpu.SemaphoreType.DMA((2 + PIECES,)))
    return pl.pallas_call(
        lambda *refs: tail_body(more, *refs),
        grid_spec=pltpu.PrefetchScalarGridSpec(
            num_scalar_prefetch=2,
            in_specs=[VMEM] * (9 + 2 * PIECES),
            out_specs=out_specs,
            scratch_shapes=scratch,
        ),
        out_shape=out_shape,
        compiler_params=params(12),
        cost_estimate=cost(1_000_000_000, 10_000_000),
        name="tail",
    )(*lists, *got, sent_c, top, basis_t, trans2, leaf_couple, *kept, *partial)


def swapped(value, mask):
    return lax.ppermute(value, "leaf", [(i, i ^ mask) for i in range(lax.axis_size("leaf"))])


def swapped_odd(value):
    size = lax.axis_size("leaf")
    pairs = [(i, i + 1) for i in range(1, size - 1, 2)]
    return lax.ppermute(value, "leaf", pairs + [(j, i) for i, j in pairs])


def one_product(node, va, vb, coef, got_va, got_vb, fill, tables):
    levels = lax.axis_size("leaf").bit_length() - 1
    top = jnp.zeros_like(node)
    got_ca = got_cb = None
    for t in range(levels):
        mask = (1 << t) if t % 2 == 0 else 3 << (t - 1)
        other = swapped(node, mask)
        fill(t)
        up, down = tables()
        if t == 0:
            va, coef, other = lax.optimization_barrier((va, coef, other))
            if got_va is None:
                got_va = swapped(va, 1)
            got_ca = swapped(coef, 1)
        if t == 3:
            vb, later, other = lax.optimization_barrier((vb, coef, other))
            if got_vb is None:
                got_vb = swapped_odd(vb)
            got_cb = swapped_odd(later)
        if t + 1 < levels:
            node = exact(node, up[t, 0]) + exact(other, up[t, 1])
        top += exact(other, down[t], NT)
    return top, (got_va, got_vb, got_ca, got_cb)


def on_device(
    rhs_block,
    basis_t,
    near_blocks,
    near_list,
    leaf_transfer,
    couple_list,
    leaf_couple,
    top_transfer,
    top_couple,
):
    leaves, rank, _ = leaf_transfer.shape
    trans2 = leaf_transfer.reshape(leaves * rank, rank)
    near_list_t, couple_list_t = near_list.T, couple_list.T
    made = {}
    kept, partial = [], []

    def fill_first(t):
        if t == 0:
            made["up"], made["down"], made["plan"], block = table(
                top_transfer, top_couple, near_list_t, near_blocks
            )
            kept.append(block)
        elif t <= PIECES:
            piece = t - 1
            out = near_piece(
                piece, near_list_t, rhs_block, near_blocks, kept[piece], piece + 1 < PIECES
            )
            partial.append(out[0])
            kept.extend(out[1:])

    def tables():
        return made["up"], made["down"]

    va, vb = split(rhs_block)
    got_va = swapped(va, 1)
    got_vb = swapped_odd(vb)
    coef, node = head(va, vb, basis_t, trans2)
    top, got = one_product(node, va, vb, coef, got_va, got_vb, fill_first, tables)
    lists = (made["plan"], couple_list_t)
    first_image, own_v, va, vb, coef_next, node = tail(
        True, lists, got, coef, top, kept, partial, basis_t, trans2, leaf_couple
    )
    again = []

    def fill_second(t):
        if t < PIECES:
            (out,) = near_piece(t, near_list_t, own_v, near_blocks, kept[t], False)
            again.append(out)

    top, got = one_product(node, va, vb, coef_next, None, None, fill_second, tables)
    (second_image,) = tail(
        False, lists, got, coef_next, top, kept, again, basis_t, trans2, leaf_couple
    )
    return (first_image, second_image)


def solution(mesh):
    in_specs = (
        P("rhs", "leaf"),
        P("leaf", None, None),
        P("leaf", None, None, None),
        P("leaf", None),
        P("leaf", None, None),
        P("leaf", None),
        P("leaf", None, None, None),
        P(),
        P(),
    )
    out_specs = (P("rhs", "leaf"), P("rhs", "leaf"))
    return jax.shard_map(
        on_device, mesh=mesh, in_specs=in_specs, out_specs=out_specs, check_vma=False
    )
```

```python
import jax
import jax.numpy as jnp
from jax import lax
from jax.experimental import pallas as pl
from jax.experimental.pallas import tpu as pltpu
from jax.sharding import PartitionSpec as P


REACH = 16
FARR = 32
PIECES = 4
TOGETHER = 8
COUNT = 144
BF = jnp.bfloat16
F32 = jnp.float32
NT = (((1,), (1,)), ((), ()))
NN = (((1,), (0,)), ((), ()))
HBM = pl.BlockSpec(memory_space=pltpu.HBM)
VMEM = pl.BlockSpec(memory_space=pltpu.VMEM)


def mm(a, b, dims=NN):
    return lax.dot_general(a, b, dims, preferred_element_type=F32)


def exact(a, b, dims=NN):
    return lax.dot_general(
        a, b, dims, precision=lax.Precision.HIGHEST, preferred_element_type=F32
    )


def params(mib):
    return pltpu.CompilerParams(vmem_limit_bytes=mib * 2**20)


def cost(flops, moved):
    return pl.CostEstimate(flops=flops, bytes_accessed=moved, transcendentals=0)


def paired_coef(v, even_basis, odd_basis):
    zero = jnp.zeros_like(even_basis)
    blocks = jnp.concatenate(
        [
            jnp.concatenate([even_basis, zero], axis=1),
            jnp.concatenate([zero, odd_basis], axis=1),
        ],
        axis=0,
    )
    return mm(v, blocks, NT).astype(BF)


def is_even():
    return (lax.axis_index("leaf") & 1) == 0


def columns_of(start, width):
    return pl.ds(pl.multiple_of(start, width), width)


def split_body(v, va, vb, sems):
    half = va.shape[1]
    start_a = jnp.where(is_even(), half, 0)
    copies = [
        pltpu.make_async_copy(v.at[:, columns_of(start, half)], out, sems.at[i])
        for i, (out, start) in enumerate(((va, start_a), (vb, half - start_a)))
    ]
    for copy in copies:
        copy.start()
    for copy in copies:
        copy.wait()


def split(vectors):
    columns, own = vectors.shape
    return pl.pallas_call(
        split_body,
        in_specs=[HBM],
        out_specs=[VMEM] * 2,
        out_shape=[jax.ShapeDtypeStruct((columns, own // 2), BF)] * 2,
        scratch_shapes=[pltpu.SemaphoreType.DMA((2,))],
        compiler_params=params(4),
        cost_estimate=cost(0, 2_000_000),
        name="split",
    )(pltpu.with_memory_space_constraint(vectors, pltpu.HBM))


def head_body(va, vb, basis_hbm, trans_hbm, coef, node, basis, trans, sems):
    leaves, rank, points = basis.shape
    first_a = jnp.where(is_even(), leaves // 2, 0)
    copies = [
        pltpu.make_async_copy(basis_hbm, basis, sems.at[0]),
        pltpu.make_async_copy(trans_hbm, trans, sems.at[1]),
    ]
    for copy in copies:
        copy.start()
    for copy in copies:
        copy.wait()
    total = None
    for v, first in ((va, first_a), (vb, leaves // 2 - first_a)):
        for pair in range(leaves // 4):
            leaf = first + 2 * pair
            rows = v[:, 2 * pair * points : 2 * (pair + 1) * points]
            both = paired_coef(rows, basis[leaf], basis[leaf + 1])
            at = columns_of((first // 2 + pair) * 2 * rank, 2 * rank)
            coef[:, at] = both
            term = mm(both, trans[at, :])
            total = term if total is None else total + term
    node[...] = total


def head(va, vb, basis_t, trans2):
    columns = va.shape[0]
    leaves, rank, _ = basis_t.shape
    hbm = (pltpu.with_memory_space_constraint(x, pltpu.HBM) for x in (basis_t, trans2))
    return pl.pallas_call(
        head_body,
        in_specs=[VMEM] * 2 + [HBM] * 2,
        out_specs=[VMEM] * 2,
        out_shape=[
            jax.ShapeDtypeStruct((columns, leaves * rank), BF),
            jax.ShapeDtypeStruct((columns, rank), F32),
        ],
        scratch_shapes=[
            pltpu.VMEM(basis_t.shape, BF),
            pltpu.VMEM(trans2.shape, BF),
            pltpu.SemaphoreType.DMA((2,)),
        ],
        compiler_params=params(6),
        cost_estimate=cost(200_000_000, 6_000_000),
        name="head",
    )(va, vb, *hbm)


def load_piece(near, kept, piece, sems):
    some = kept.shape[0] // PIECES
    return [
        pltpu.make_async_copy(near.at[piece * some + i], kept.at[piece * some + i], sems.at[i])
        for i in range(some)
    ]


def table_body(levels, near_list, trans_hbm, couple_hbm, near, up, pair, plan, kept, *scratch):
    trans, couple, sems = scratch
    copies = [
        pltpu.make_async_copy(trans_hbm, trans, sems.at[8]),
        pltpu.make_async_copy(couple_hbm, couple, sems.at[9]),
    ]
    copies += load_piece(near, kept, 0, sems)
    for copy in copies:
        copy.start()
    device = lax.axis_index("leaf")
    kn, leaves = near_list.shape
    first = device * leaves

    def scan(leaf, n):
        for slot in range(kn):
            source = near_list[slot, leaf] - first
            left = source < 0
            place = source + jnp.where(left, REACH, REACH - leaves)
            plan[n] = (leaf * 8 + slot) * 32 + place
            n = n + jnp.where(left | (source >= leaves), 1, 0)
        return n

    total = lax.fori_loop(0, leaves, scan, 0)
    for i in range(TOGETHER):
        plan[total + i] = (leaves * 8) * 32
    plan[COUNT] = lax.div(total + TOGETHER - 1, TOGETHER)
    count, rows, nodes = 8, trans.shape[0], trans.shape[2]
    row = lax.broadcasted_iota(jnp.int32, (count, nodes), 0)
    node = lax.broadcasted_iota(jnp.int32, (count, nodes), 1)
    offset = (2 << levels) - lax.shift_right_logical(jnp.full_like(row, 2 << levels), row)
    here = offset + lax.shift_right_logical(jnp.zeros_like(row) + device, row)
    there = jnp.bitwise_xor(here, 1)
    wanted = row < levels
    pick_here = jnp.where(wanted & (node == here), 1.0, 0.0).astype(BF)
    pick_there = jnp.where(wanted & (node == there), 1.0, 0.0).astype(BF)
    both = jnp.concatenate([pick_here, pick_there], axis=0)
    copies[0].wait()
    copies[1].wait()
    for k in range(rows):
        picked = mm(both, trans[k], NT)
        up[0, :, k, :] = picked[:levels]
        up[1, :, k, :] = picked[count : count + levels]
        pair[:, k, :] = mm(pick_here, couple[k], NT)[:levels]
    for copy in copies[2:]:
        copy.wait()


def chain_body(up, pair, down):
    levels = pair.shape[0]
    down[0] = pair[0]
    path = up[0, 0]
    for t in range(1, levels):
        down[t] = exact(path, pair[t])
        if t + 1 < levels:
            path = exact(path, up[0, t])


def chain(up, pair):
    return pl.pallas_call(
        chain_body,
        in_specs=[VMEM] * 2,
        out_specs=VMEM,
        out_shape=jax.ShapeDtypeStruct(pair.shape, F32),
        compiler_params=params(4),
        cost_estimate=cost(10_000_000, 1_000_000),
        name="chain",
    )(up, pair)


def table(top_transfer, top_couple, near_list_t, near_blocks):
    nodes, rank, _ = top_transfer.shape
    levels = lax.axis_size("leaf").bit_length() - 1
    shape = near_blocks.shape
    hbm = (
        jnp.transpose(top_transfer, (1, 2, 0)),
        jnp.transpose(top_couple, (1, 2, 0)),
        near_blocks,
    )
    return pl.pallas_call(
        lambda *refs: table_body(levels, *refs),
        grid_spec=pltpu.PrefetchScalarGridSpec(
            num_scalar_prefetch=1,
            in_specs=[HBM] * 3,
            out_specs=[VMEM, VMEM, pl.BlockSpec(memory_space=pltpu.SMEM), VMEM],
            scratch_shapes=[
                pltpu.VMEM((rank, rank, nodes), BF),
                pltpu.VMEM((rank, rank, nodes), BF),
                pltpu.SemaphoreType.DMA((shape[0] // PIECES + 2,)),
            ],
        ),
        out_shape=[
            jax.ShapeDtypeStruct((2, levels, rank, rank), F32),
            jax.ShapeDtypeStruct((levels, rank, rank), F32),
            jax.ShapeDtypeStruct((COUNT + 8,), jnp.int32),
            jax.ShapeDtypeStruct(shape, BF),
        ],
        compiler_params=params(6),
        cost_estimate=cost(10_000_000, 8_000_000),
        name="table",
    )(near_list_t, *(pltpu.with_memory_space_constraint(x, pltpu.HBM) for x in hbm))


def near_body(piece, load, near_list, v, kept, *refs):
    copies = []
    if load:
        near, total, kept, sems = refs
        copies = load_piece(near, kept, piece + 1, sems)
        for copy in copies:
            copy.start()
    else:
        (total,) = refs
    leaves, kn, points, _ = kept.shape
    some = leaves // PIECES
    first = lax.axis_index("leaf") * leaves
    for i in range(some):
        out = None
        leaf = piece * some + i
        for s in range(kn):
            source = near_list[s, leaf] - first
            inside = (source >= 0) & (source < leaves)
            rows = v[:, columns_of(jnp.clip(source, 0, leaves - 1) * points, points)]
            term = mm(jnp.where(inside, rows, jnp.zeros_like(rows)), kept[leaf, s], NT)
            out = term if out is None else out + term
        total[:, i * points : (i + 1) * points] = out
    for copy in copies:
        copy.wait()


def near_piece(piece, near_list_t, v, near_blocks, kept, load):
    columns = v.shape[0]
    leaves, _, points, _ = kept.shape
    some = leaves // PIECES
    in_specs = [VMEM, VMEM]
    args = [v, kept]
    out_shape = [jax.ShapeDtypeStruct((columns, some * points), F32)]
    scratch = []
    if load:
        in_specs.append(HBM)
        args.append(pltpu.with_memory_space_constraint(near_blocks, pltpu.HBM))
        out_shape.append(jax.ShapeDtypeStruct(kept.shape, BF))
        scratch.append(pltpu.SemaphoreType.DMA((some,)))
    return pl.pallas_call(
        lambda *refs: near_body(piece, load, *refs),
        grid_spec=pltpu.PrefetchScalarGridSpec(
            num_scalar_prefetch=1,
            in_specs=in_specs,
            out_specs=[VMEM] * len(out_shape),
            scratch_shapes=scratch,
        ),
        out_shape=out_shape,
        input_output_aliases={2: 1} if load else {},
        compiler_params=params(4),
        cost_estimate=cost(350_000_000, 6_000_000),
    )(near_list_t, *args)


def tail_body(more, plan, couple_list, *refs):
    got_va, got_vb, got_ca, got_cb, sent_c, top, basis, trans, couple = refs[:9]
    refs = refs[9:]
    near, partial, refs = refs[0], refs[1 : 1 + PIECES], refs[1 + PIECES :]
    if more:
        image, own_v, va, vb, coef, node, table_ref, wide, acc, total_ref, sems = refs
    else:
        image, own_v, table_ref, wide, acc, sems = refs
    leaves, rank, points = basis.shape
    some = leaves // PIECES
    half = leaves // 2 * points
    even = is_even()
    first = lax.axis_index("leaf") * leaves
    start_a = jnp.where(even, half, 0)
    copies = [
        pltpu.make_async_copy(ref, wide.at[:, columns_of(start, half)], sems.at[i])
        for i, (ref, start) in enumerate(((got_va, start_a), (got_vb, half - start_a)))
    ]
    for copy in copies:
        copy.start()
    row = lax.broadcasted_iota(jnp.int32, (2 * rank, 2 * rank), 0)
    lane = lax.broadcasted_iota(jnp.int32, (2 * rank, 2 * rank), 1)
    swap = jnp.where(jnp.bitwise_xor(row, rank) == lane, 1.0, 0.0).astype(BF)
    base_a = jnp.where(even, 2 * leaves, 0)
    for ref, base in ((got_ca, base_a), (sent_c, leaves), (got_cb, 2 * leaves - base_a)):
        for pair in range(leaves // 2):
            both = ref[:, 2 * rank * pair : 2 * rank * (pair + 1)]
            table_ref[base + 2 * pair] = both
            table_ref[base + 2 * pair + 1] = mm(both, swap).astype(BF)
    descent = top[...].astype(BF)
    if more:
        total_ref[...] = jnp.zeros_like(total_ref)
    for piece in range(PIECES):
        width = some * points
        acc[:, piece * width : (piece + 1) * width] = partial[piece][...]
    for copy in copies:
        copy.wait()

    def add(j, carry):
        terms = []
        for i in range(TOGETHER):
            code = plan[j * TOGETHER + i]
            leaf = lax.shift_right_logical(code, 8)
            slot = lax.shift_right_logical(code, 5) & 7
            rows = wide[:, columns_of((code & 31) * points, points)]
            term = mm(rows, near[leaf & (leaves - 1), slot], NT)
            terms.append((columns_of(leaf * points, points), term))
        for here, term in terms:
            acc[:, here] += term
        return carry

    lax.fori_loop(0, plan[COUNT], add, 0)
    writes = []
    for piece in range(PIECES):
        results = []
        for i in range(some):
            leaf = piece * some + i
            moved = trans[leaf * rank : (leaf + 1) * rank, :]
            local = mm(descent, moved, NT)
            for s in range(couple.shape[1]):
                source = couple_list[s, leaf] - first + FARR
                local += mm(table_ref[source, :, :rank], couple[leaf, s], NT)
            here = slice(leaf * points, (leaf + 1) * points)
            value = (acc[:, here] + mm(local.astype(BF), basis[leaf])).astype(BF)
            results.append(value)
            own_v[:, here] = value
        here = pl.ds(piece * some * points, some * points)
        writes.append(pltpu.make_async_copy(own_v.at[:, here], image.at[:, here], sems.at[2 + piece]))
        writes[-1].start()
        if not more:
            continue
        for pair in range(some // 2):
            leaf = piece * some + 2 * pair
            rows = jnp.concatenate(results[2 * pair : 2 * pair + 2], axis=1)
            both = paired_coef(rows, basis[leaf], basis[leaf + 1])
            coef[:, leaf * rank : (leaf + 2) * rank] = both
            total_ref[...] += mm(both, trans[leaf * rank : (leaf + 2) * rank, :])
        in_right = piece >= PIECES // 2
        start = piece % (PIECES // 2) * some * points

        def put(message, results=results, start=start):
            for i, value in enumerate(results):
                message[:, start + i * points : start + (i + 1) * points] = value

        @pl.when(even == in_right)
        def _():
            put(va)

        @pl.when(even != in_right)
        def _():
            put(vb)

    if more:
        node[...] = total_ref[...]
    for write in writes:
        write.wait()


def tail(more, lists, got, sent_c, top, kept, partial, basis_t, trans2, leaf_couple):
    columns = sent_c.shape[0]
    leaves, rank, points = basis_t.shape
    own = leaves * points
    image = jax.ShapeDtypeStruct((columns, own), BF)
    out_shape, out_specs = [image], [HBM]
    scratch = [
        pltpu.VMEM((3 * leaves, columns, 2 * rank), BF),
        pltpu.VMEM((columns, own), BF),
        pltpu.VMEM((columns, own + points), F32),
    ]
    if more:
        half = jax.ShapeDtypeStruct((columns, own // 2), BF)
        out_shape += [
            image,
            half,
            half,
            jax.ShapeDtypeStruct((columns, leaves * rank), BF),
            jax.ShapeDtypeStruct((columns, rank), F32),
        ]
        out_specs += [VMEM] * 5
        scratch.append(pltpu.VMEM((columns, rank), F32))
    else:
        scratch.insert(0, pltpu.VMEM((columns, own), BF))
    scratch.append(pltpu.SemaphoreType.DMA((2 + PIECES,)))
    return pl.pallas_call(
        lambda *refs: tail_body(more, *refs),
        grid_spec=pltpu.PrefetchScalarGridSpec(
            num_scalar_prefetch=2,
            in_specs=[VMEM] * (10 + PIECES),
            out_specs=out_specs,
            scratch_shapes=scratch,
        ),
        out_shape=out_shape,
        compiler_params=params(12),
        cost_estimate=cost(1_000_000_000, 10_000_000),
        name="tail",
    )(*lists, *got, sent_c, top, basis_t, trans2, leaf_couple, kept, *partial)


def swapped(value, mask):
    return lax.ppermute(value, "leaf", [(i, i ^ mask) for i in range(lax.axis_size("leaf"))])


def swapped_odd(value):
    size = lax.axis_size("leaf")
    pairs = [(i, i + 1) for i in range(1, size - 1, 2)]
    return lax.ppermute(value, "leaf", pairs + [(j, i) for i, j in pairs])


def one_product(node, va, vb, coef, got_va, got_vb, fill, tables):
    levels = lax.axis_size("leaf").bit_length() - 1
    top = jnp.zeros_like(node)
    got_ca = got_cb = None
    others = []
    for t in range(levels):
        mask = (1 << t) if t % 2 == 0 else 3 << (t - 1)
        other = swapped(node, mask)
        fill(t)
        up, down = tables(t)
        if t == 0:
            va, coef, other = lax.optimization_barrier((va, coef, other))
            if got_va is None:
                got_va = swapped(va, 1)
            got_ca = swapped(coef, 1)
        if t == 3:
            vb, later, other = lax.optimization_barrier((vb, coef, other))
            if got_vb is None:
                got_vb = swapped_odd(vb)
            got_cb = swapped_odd(later)
        if t + 1 < levels:
            node = exact(node, up[0, t]) + exact(other, up[1, t])
        others.append(other)
    for t, other in enumerate(others):
        top += exact(other, down[t], NT)
    return top, (got_va, got_vb, got_ca, got_cb)


def on_device(
    rhs_block,
    basis_t,
    near_blocks,
    near_list,
    leaf_transfer,
    couple_list,
    leaf_couple,
    top_transfer,
    top_couple,
):
    leaves, rank, _ = leaf_transfer.shape
    trans2 = leaf_transfer.reshape(leaves * rank, rank)
    near_list_t, couple_list_t = near_list.T, couple_list.T
    made = {}
    partial = []

    def fill_first(t):
        if t == 0:
            made["up"], made["pair"], made["plan"], made["kept"] = table(
                top_transfer, top_couple, near_list_t, near_blocks
            )
        elif t <= PIECES:
            load = t < PIECES
            out = near_piece(t - 1, near_list_t, rhs_block, near_blocks, made["kept"], load)
            partial.append(out[0])
            if load:
                made["kept"] = out[1]

    def tables(t):
        if t == 4 and "down" not in made:
            made["down"] = chain(made["up"], made["pair"])
        return made["up"], made.get("down")

    va, vb = split(rhs_block)
    got_va = swapped(va, 1)
    got_vb = swapped_odd(vb)
    coef, node = head(va, vb, basis_t, trans2)
    top, got = one_product(node, va, vb, coef, got_va, got_vb, fill_first, tables)
    lists = (made["plan"], couple_list_t)
    first_image, own_v, va, vb, coef_next, node = tail(
        True, lists, got, coef, top, made["kept"], partial, basis_t, trans2, leaf_couple
    )
    again = []

    def fill_second(t):
        if t == 4:
            for piece in range(PIECES):
                (out,) = near_piece(piece, near_list_t, own_v, near_blocks, made["kept"], False)
                again.append(out)

    top, got = one_product(node, va, vb, coef_next, None, None, fill_second, tables)
    (second_image,) = tail(
        False, lists, got, coef_next, top, made["kept"], again, basis_t, trans2, leaf_couple
    )
    return (first_image, second_image)


def solution(mesh):
    in_specs = (
        P("rhs", "leaf"),
        P("leaf", None, None),
        P("leaf", None, None, None),
        P("leaf", None),
        P("leaf", None, None),
        P("leaf", None),
        P("leaf", None, None, None),
        P(),
        P(),
    )
    out_specs = (P("rhs", "leaf"), P("rhs", "leaf"))
    return jax.shard_map(
        on_device, mesh=mesh, in_specs=in_specs, out_specs=out_specs, check_vma=False
    )
```

```python
import jax
import jax.numpy as jnp
from jax import lax
from jax.experimental import pallas as pl
from jax.experimental.pallas import tpu as pltpu
from jax.sharding import PartitionSpec as P


REACH = 16
FARR = 32
PIECES = 4
TOGETHER = 8
LIST = 80
BF = jnp.bfloat16
F32 = jnp.float32
NT = (((1,), (1,)), ((), ()))
NN = (((1,), (0,)), ((), ()))
HBM = pl.BlockSpec(memory_space=pltpu.HBM)
VMEM = pl.BlockSpec(memory_space=pltpu.VMEM)


def mm(a, b, dims=NN):
    return lax.dot_general(a, b, dims, preferred_element_type=F32)


def exact(a, b, dims=NN):
    return lax.dot_general(
        a, b, dims, precision=lax.Precision.HIGHEST, preferred_element_type=F32
    )


def params(mib):
    return pltpu.CompilerParams(vmem_limit_bytes=mib * 2**20)


def cost(flops, moved):
    return pl.CostEstimate(flops=flops, bytes_accessed=moved, transcendentals=0)


def paired_coef(v, even_basis, odd_basis):
    zero = jnp.zeros_like(even_basis)
    blocks = jnp.concatenate(
        [
            jnp.concatenate([even_basis, zero], axis=1),
            jnp.concatenate([zero, odd_basis], axis=1),
        ],
        axis=0,
    )
    return mm(v, blocks, NT).astype(BF)


def is_even():
    return (lax.axis_index("leaf") & 1) == 0


def columns_of(start, width):
    return pl.ds(pl.multiple_of(start, width), width)


def split_body(v, va, vb, sems):
    half = va.shape[1]
    start_a = jnp.where(is_even(), half, 0)
    copies = [
        pltpu.make_async_copy(v.at[:, columns_of(start, half)], out, sems.at[i])
        for i, (out, start) in enumerate(((va, start_a), (vb, half - start_a)))
    ]
    for copy in copies:
        copy.start()
    for copy in copies:
        copy.wait()


def split(vectors):
    columns, own = vectors.shape
    return pl.pallas_call(
        split_body,
        in_specs=[HBM],
        out_specs=[VMEM] * 2,
        out_shape=[jax.ShapeDtypeStruct((columns, own // 2), BF)] * 2,
        scratch_shapes=[pltpu.SemaphoreType.DMA((2,))],
        compiler_params=params(4),
        cost_estimate=cost(0, 2_000_000),
        name="split",
    )(pltpu.with_memory_space_constraint(vectors, pltpu.HBM))


def head_body(va, vb, basis_hbm, trans_hbm, coef, node, basis, trans, sems):
    leaves, rank, points = basis.shape
    first_a = jnp.where(is_even(), leaves // 2, 0)
    copies = [
        pltpu.make_async_copy(basis_hbm, basis, sems.at[0]),
        pltpu.make_async_copy(trans_hbm, trans, sems.at[1]),
    ]
    for copy in copies:
        copy.start()
    for copy in copies:
        copy.wait()
    total = None
    for v, first in ((va, first_a), (vb, leaves // 2 - first_a)):
        for pair in range(leaves // 4):
            leaf = first + 2 * pair
            rows = v[:, 2 * pair * points : 2 * (pair + 1) * points]
            both = paired_coef(rows, basis[leaf], basis[leaf + 1])
            at = columns_of((first // 2 + pair) * 2 * rank, 2 * rank)
            coef[:, at] = both
            term = mm(both, trans[at, :])
            total = term if total is None else total + term
    node[...] = total


def head(va, vb, basis_t, trans2):
    columns = va.shape[0]
    leaves, rank, _ = basis_t.shape
    hbm = (pltpu.with_memory_space_constraint(x, pltpu.HBM) for x in (basis_t, trans2))
    return pl.pallas_call(
        head_body,
        in_specs=[VMEM] * 2 + [HBM] * 2,
        out_specs=[VMEM] * 2,
        out_shape=[
            jax.ShapeDtypeStruct((columns, leaves * rank), BF),
            jax.ShapeDtypeStruct((columns, rank), F32),
        ],
        scratch_shapes=[
            pltpu.VMEM(basis_t.shape, BF),
            pltpu.VMEM(trans2.shape, BF),
            pltpu.SemaphoreType.DMA((2,)),
        ],
        compiler_params=params(6),
        cost_estimate=cost(200_000_000, 6_000_000),
        name="head",
    )(va, vb, *hbm)


def load_piece(near, kept, piece, sems):
    some = kept.shape[0] // PIECES
    return [
        pltpu.make_async_copy(near.at[piece * some + i], kept.at[piece * some + i], sems.at[i])
        for i in range(some)
    ]


def table_body(levels, near_list, trans_hbm, couple_hbm, near, up, pair, plan, kept, *scratch):
    trans, couple, sems = scratch
    copies = [
        pltpu.make_async_copy(trans_hbm, trans, sems.at[8]),
        pltpu.make_async_copy(couple_hbm, couple, sems.at[9]),
    ]
    copies += load_piece(near, kept, 0, sems)
    for copy in copies:
        copy.start()
    device = lax.axis_index("leaf")
    kn, leaves = near_list.shape
    first = device * leaves
    even = is_even()

    def scan(leaf, found):
        in_a, in_b = found
        for slot in range(kn):
            source = near_list[slot, leaf] - first
            left = source < 0
            outside = left | (source >= leaves)
            to_a = left != even
            code = (leaf * 8 + slot) * 16 + source + jnp.where(left, REACH, -leaves)
            plan[in_a] = code
            plan[LIST + in_b] = code
            in_a = in_a + jnp.where(outside & to_a, 1, 0)
            in_b = in_b + jnp.where(outside & jnp.logical_not(to_a), 1, 0)
        return in_a, in_b

    found = lax.fori_loop(0, leaves, scan, (jnp.int32(0), jnp.int32(0)))
    for side, total in enumerate(found):
        for i in range(TOGETHER):
            plan[side * LIST + total + i] = (leaves * 8) * 16
        plan[2 * LIST + side] = lax.div(total + TOGETHER - 1, TOGETHER)
    count, rows, nodes = 8, trans.shape[0], trans.shape[2]
    row = lax.broadcasted_iota(jnp.int32, (count, nodes), 0)
    node = lax.broadcasted_iota(jnp.int32, (count, nodes), 1)
    offset = (2 << levels) - lax.shift_right_logical(jnp.full_like(row, 2 << levels), row)
    here = offset + lax.shift_right_logical(jnp.zeros_like(row) + device, row)
    there = jnp.bitwise_xor(here, 1)
    wanted = row < levels
    pick_here = jnp.where(wanted & (node == here), 1.0, 0.0).astype(BF)
    pick_there = jnp.where(wanted & (node == there), 1.0, 0.0).astype(BF)
    both = jnp.concatenate([pick_here, pick_there], axis=0)
    copies[0].wait()
    copies[1].wait()
    for k in range(rows):
        picked = mm(both, trans[k], NT)
        up[0, :, k, :] = picked[:levels]
        up[1, :, k, :] = picked[count : count + levels]
        pair[:, k, :] = mm(pick_here, couple[k], NT)[:levels]
    for copy in copies[2:]:
        copy.wait()


def chain_body(up, pair, down):
    levels = pair.shape[0]
    down[0] = pair[0]
    path = up[0, 0]
    for t in range(1, levels):
        down[t] = exact(path, pair[t])
        if t + 1 < levels:
            path = exact(path, up[0, t])


def chain(up, pair):
    return pl.pallas_call(
        chain_body,
        in_specs=[VMEM] * 2,
        out_specs=VMEM,
        out_shape=jax.ShapeDtypeStruct(pair.shape, F32),
        compiler_params=params(4),
        cost_estimate=cost(10_000_000, 1_000_000),
        name="chain",
    )(up, pair)


def table(top_transfer, top_couple, near_list_t, near_blocks):
    nodes, rank, _ = top_transfer.shape
    levels = lax.axis_size("leaf").bit_length() - 1
    shape = near_blocks.shape
    hbm = (
        jnp.transpose(top_transfer, (1, 2, 0)),
        jnp.transpose(top_couple, (1, 2, 0)),
        near_blocks,
    )
    return pl.pallas_call(
        lambda *refs: table_body(levels, *refs),
        grid_spec=pltpu.PrefetchScalarGridSpec(
            num_scalar_prefetch=1,
            in_specs=[HBM] * 3,
            out_specs=[VMEM, VMEM, pl.BlockSpec(memory_space=pltpu.SMEM), VMEM],
            scratch_shapes=[
                pltpu.VMEM((rank, rank, nodes), BF),
                pltpu.VMEM((rank, rank, nodes), BF),
                pltpu.SemaphoreType.DMA((shape[0] // PIECES + 2,)),
            ],
        ),
        out_shape=[
            jax.ShapeDtypeStruct((2, levels, rank, rank), F32),
            jax.ShapeDtypeStruct((levels, rank, rank), F32),
            jax.ShapeDtypeStruct((2 * LIST + 8,), jnp.int32),
            jax.ShapeDtypeStruct(shape, BF),
        ],
        compiler_params=params(6),
        cost_estimate=cost(10_000_000, 8_000_000),
        name="table",
    )(near_list_t, *(pltpu.with_memory_space_constraint(x, pltpu.HBM) for x in hbm))


def near_body(piece, load, near_list, v, kept, *refs):
    copies = []
    if load:
        near, total, kept, sems = refs
        copies = load_piece(near, kept, piece + 1, sems)
        for copy in copies:
            copy.start()
    else:
        (total,) = refs
    leaves, kn, points, _ = kept.shape
    some = leaves // PIECES
    first = lax.axis_index("leaf") * leaves
    for i in range(some):
        out = None
        leaf = piece * some + i
        for s in range(kn):
            source = near_list[s, leaf] - first
            inside = (source >= 0) & (source < leaves)
            rows = v[:, columns_of(jnp.clip(source, 0, leaves - 1) * points, points)]
            term = mm(jnp.where(inside, rows, jnp.zeros_like(rows)), kept[leaf, s], NT)
            out = term if out is None else out + term
        total[:, i * points : (i + 1) * points] = out
    for copy in copies:
        copy.wait()


def near_piece(piece, near_list_t, v, near_blocks, kept, load):
    columns = v.shape[0]
    leaves, _, points, _ = kept.shape
    some = leaves // PIECES
    in_specs = [VMEM, VMEM]
    args = [v, kept]
    out_shape = [jax.ShapeDtypeStruct((columns, some * points), F32)]
    scratch = []
    if load:
        in_specs.append(HBM)
        args.append(pltpu.with_memory_space_constraint(near_blocks, pltpu.HBM))
        out_shape.append(jax.ShapeDtypeStruct(kept.shape, BF))
        scratch.append(pltpu.SemaphoreType.DMA((some,)))
    return pl.pallas_call(
        lambda *refs: near_body(piece, load, *refs),
        grid_spec=pltpu.PrefetchScalarGridSpec(
            num_scalar_prefetch=1,
            in_specs=in_specs,
            out_specs=[VMEM] * len(out_shape),
            scratch_shapes=scratch,
        ),
        out_shape=out_shape,
        input_output_aliases={2: 1} if load else {},
        compiler_params=params(4),
        cost_estimate=cost(350_000_000, 6_000_000),
    )(near_list_t, *args)


def add_halo(side, plan, v, near, acc):
    leaves, _, points, _ = near.shape

    def add(j, carry):
        terms = []
        for i in range(TOGETHER):
            code = plan[side * LIST + j * TOGETHER + i]
            leaf = lax.shift_right_logical(code, 7)
            slot = lax.shift_right_logical(code, 4) & 7
            rows = v[:, columns_of((code & 15) * points, points)]
            term = mm(rows, near[leaf & (leaves - 1), slot], NT)
            terms.append((columns_of(leaf * points, points), term))
        for here, term in terms:
            acc[:, here] += term
        return carry

    lax.fori_loop(0, plan[2 * LIST + side], add, 0)


def unpack(coef, base, table_ref):
    wide = table_ref.shape[2]
    row = lax.broadcasted_iota(jnp.int32, (wide, wide), 0)
    lane = lax.broadcasted_iota(jnp.int32, (wide, wide), 1)
    swap = jnp.where(jnp.bitwise_xor(row, wide // 2) == lane, 1.0, 0.0).astype(BF)
    for pair in range(coef.shape[1] // wide):
        both = coef[:, wide * pair : wide * (pair + 1)]
        table_ref[base + 2 * pair] = both
        table_ref[base + 2 * pair + 1] = mm(both, swap).astype(BF)


def side_body(plan, got_va, got_ca, sent_c, near, *refs):
    partial, (acc, table_ref) = refs[:PIECES], refs[PIECES:]
    leaves = near.shape[0]
    for piece, part in enumerate(partial):
        width = part.shape[1]
        acc[:, piece * width : (piece + 1) * width] = part[...]
    unpack(sent_c, leaves, table_ref)
    unpack(got_ca, jnp.where(is_even(), 2 * leaves, 0), table_ref)
    add_halo(0, plan, got_va, near, acc)


def side_a(plan, got_va, got_ca, sent_c, kept, partial):
    columns = sent_c.shape[0]
    leaves, _, points, _ = kept.shape
    rank = sent_c.shape[1] // leaves
    return pl.pallas_call(
        side_body,
        grid_spec=pltpu.PrefetchScalarGridSpec(
            num_scalar_prefetch=1,
            in_specs=[VMEM] * (4 + PIECES),
            out_specs=[VMEM] * 2,
        ),
        out_shape=[
            jax.ShapeDtypeStruct((columns, (leaves + 1) * points), F32),
            jax.ShapeDtypeStruct((3 * leaves, columns, 2 * rank), BF),
        ],
        compiler_params=params(4),
        cost_estimate=cost(400_000_000, 6_000_000),
        name="side",
    )(plan, got_va, got_ca, sent_c, kept, *partial)


def tail_body(names, sides, more, *refs):
    r = dict(zip(names, refs))
    acc, table_ref, couple_list = r["acc"], r["table"], r["couple_list"]
    basis, trans, couple, image = r["basis"], r["trans"], r["couple"], r["image"]
    leaves, rank, points = basis.shape
    group = leaves // 4
    even = is_even()
    first = lax.axis_index("leaf") * leaves
    first_b = jnp.where(even, 0, leaves // 2)
    descent = r["top"][...].astype(BF)
    if "b" in sides:
        unpack(r["got_cb"], jnp.where(even, 0, 2 * leaves), table_ref)
        add_halo(1, r["plan"], r["got_vb"], r["near"], acc)
    own_v = r["own_v"]
    writes = []
    total = r["node_in"][...] if "node_in" in r else None
    for side in sides:
        start = first_b if side == "b" else leaves // 2 - first_b
        for part in range(2):
            base = start + part * group
            results = []
            for i in range(group):
                leaf = base + i
                moved = trans[columns_of(leaf * rank, rank), :]
                local = mm(descent, moved, NT)
                for s in range(couple.shape[1]):
                    source = couple_list[s, leaf] - first + FARR
                    local += mm(table_ref[source, :, :rank], couple[leaf, s], NT)
                here = columns_of(leaf * points, points)
                value = (acc[:, here] + mm(local.astype(BF), basis[leaf])).astype(BF)
                results.append(value)
                own_v[:, here] = value
                if more:
                    at = (part * group + i) * points
                    r["message"][:, at : at + points] = value
            here = columns_of(base * points, group * points)
            writes.append(
                pltpu.make_async_copy(own_v.at[:, here], image.at[:, here], r["sems"].at[len(writes)])
            )
            writes[-1].start()
            if not more:
                continue
            for pair in range(group // 2):
                leaf = base + 2 * pair
                rows = jnp.concatenate(results[2 * pair : 2 * pair + 2], axis=1)
                both = paired_coef(rows, basis[leaf], basis[leaf + 1])
                at = columns_of((base // 2 + pair) * 2 * rank, 2 * rank)
                r["coef"][:, at] = both
                term = mm(both, trans[at, :])
                total = term if total is None else total + term
    if more:
        r["node"][...] = total
    for write in writes:
        write.wait()


def tail(sides, more, scalars, inputs, carried):
    leaves, rank, points = inputs["basis"].shape
    columns = inputs["top"].shape[0]
    own = leaves * points
    fresh = {}
    if "image" not in carried:
        fresh["image"] = jax.ShapeDtypeStruct((columns, own), BF)
    if more:
        if "own_v" not in carried:
            fresh["own_v"] = jax.ShapeDtypeStruct((columns, own), BF)
            fresh["coef"] = jax.ShapeDtypeStruct((columns, leaves * rank), BF)
        fresh["message"] = jax.ShapeDtypeStruct((columns, own // 2), BF)
        fresh["node"] = jax.ShapeDtypeStruct((columns, rank), F32)
    outs = [*carried, *fresh]
    before = [*scalars, *inputs]
    names = [*before, *(f"old_{name}" for name in carried), *outs]
    scratch = [pltpu.SemaphoreType.DMA((4,))]
    names.append("sems")
    if not more:
        scratch.append(pltpu.VMEM((columns, own), BF))
        names.append("own_v")
    spec = lambda name: HBM if name == "image" else VMEM
    result = pl.pallas_call(
        lambda *refs: tail_body(names, sides, more, *refs),
        grid_spec=pltpu.PrefetchScalarGridSpec(
            num_scalar_prefetch=len(scalars),
            in_specs=[VMEM] * len(inputs) + [spec(name) for name in carried],
            out_specs=[spec(name) for name in outs],
            scratch_shapes=scratch,
        ),
        out_shape=[
            jax.ShapeDtypeStruct(carried[name].shape, carried[name].dtype)
            if name in carried
            else fresh[name]
            for name in outs
        ],
        input_output_aliases={len(before) + i: i for i in range(len(carried))},
        compiler_params=params(6),
        cost_estimate=cost(600_000_000, 6_000_000),
    )(*scalars.values(), *inputs.values(), *carried.values())
    return dict(zip(outs, result))


def swapped(value, mask):
    return lax.ppermute(value, "leaf", [(i, i ^ mask) for i in range(lax.axis_size("leaf"))])


def swapped_odd(value):
    size = lax.axis_size("leaf")
    pairs = [(i, i + 1) for i in range(1, size - 1, 2)]
    return lax.ppermute(value, "leaf", pairs + [(j, i) for i, j in pairs])


def one_product(node, va, coef, got_va, fill, tables):
    levels = lax.axis_size("leaf").bit_length() - 1
    top = jnp.zeros_like(node)
    got_ca = got_cb = None
    others = []
    for t in range(levels):
        mask = (1 << t) if t % 2 == 0 else 3 << (t - 1)
        other = swapped(node, mask)
        fill(t)
        up, down = tables(t)
        if t == 0:
            va, coef, other = lax.optimization_barrier((va, coef, other))
            if got_va is None:
                got_va = swapped(va, 1)
            got_ca = swapped(coef, 1)
        if t == 3:
            later, other = lax.optimization_barrier((coef, other))
            got_cb = swapped_odd(later)
        if t + 1 < levels:
            node = exact(node, up[0, t]) + exact(other, up[1, t])
        others.append(other)
    for t, other in enumerate(others):
        top += exact(other, down[t], NT)
    return top, got_va, got_ca, got_cb


def on_device(
    rhs_block,
    basis_t,
    near_blocks,
    near_list,
    leaf_transfer,
    couple_list,
    leaf_couple,
    top_transfer,
    top_couple,
):
    leaves, rank, _ = leaf_transfer.shape
    trans2 = leaf_transfer.reshape(leaves * rank, rank)
    near_list_t, couple_list_t = near_list.T, couple_list.T
    made = {}
    partial, again = [], []

    def fill_first(t):
        if t == 0:
            made["up"], made["pair"], made["plan"], made["kept"] = table(
                top_transfer, top_couple, near_list_t, near_blocks
            )
        elif t <= PIECES:
            load = t < PIECES
            out = near_piece(t - 1, near_list_t, rhs_block, near_blocks, made["kept"], load)
            partial.append(out[0])
            if load:
                made["kept"] = out[1]

    def tables(t):
        if t == 4 and "down" not in made:
            made["down"] = chain(made["up"], made["pair"])
        return made["up"], made.get("down")

    def fill_second(t):
        for piece in {1: (0, 1), 4: (2, 3)}.get(t, ()):
            (out,) = near_piece(piece, near_list_t, made["own_v"], near_blocks, made["kept"], False)
            again.append(out)

    def parts(top, got_vb, got_cb):
        scalars = {"plan": made["plan"], "couple_list": couple_list_t}
        inputs = {"top": top, "basis": basis_t, "trans": trans2, "couple": leaf_couple}
        on_b = {"got_vb": got_vb, "got_cb": got_cb, "near": made["kept"]}
        return scalars, inputs, on_b

    va, vb = split(rhs_block)
    got_va = swapped(va, 1)
    got_vb = swapped_odd(vb)
    coef, node = head(va, vb, basis_t, trans2)
    top, _, got_ca, got_cb = one_product(node, va, coef, got_va, fill_first, tables)
    acc, entries = side_a(made["plan"], got_va, got_ca, coef, made["kept"], partial)
    scalars, inputs, on_b = parts(top, got_vb, got_cb)
    half = tail("b", True, scalars, {**inputs, **on_b}, {"acc": acc, "table": entries})
    got_vb = swapped_odd(half["message"])
    inputs["node_in"] = half["node"]
    carried = {k: half[k] for k in ("acc", "table", "image", "own_v", "coef")}
    rest = tail("a", True, scalars, inputs, carried)
    first_image, coef, made["own_v"] = rest["image"], rest["coef"], rest["own_v"]
    top, got_va, got_ca, got_cb = one_product(
        rest["node"], rest["message"], coef, None, fill_second, tables
    )
    acc, entries = side_a(made["plan"], got_va, got_ca, coef, made["kept"], again)
    scalars, inputs, on_b = parts(top, got_vb, got_cb)
    last = tail("ba", False, scalars, {**inputs, **on_b}, {"acc": acc, "table": entries})
    return (first_image, last["image"])


def solution(mesh):
    in_specs = (
        P("rhs", "leaf"),
        P("leaf", None, None),
        P("leaf", None, None, None),
        P("leaf", None),
        P("leaf", None, None),
        P("leaf", None),
        P("leaf", None, None, None),
        P(),
        P(),
    )
    out_specs = (P("rhs", "leaf"), P("rhs", "leaf"))
    return jax.shard_map(
        on_device, mesh=mesh, in_specs=in_specs, out_specs=out_specs, check_vma=False
    )
```

```python
import jax
import jax.numpy as jnp
from jax import lax
from jax.experimental import pallas as pl
from jax.experimental.pallas import tpu as pltpu
from jax.sharding import PartitionSpec as P


REACH = 16
FARR = 32
PIECES = 4
TOGETHER = 8
LIST = 80
BF = jnp.bfloat16
F32 = jnp.float32
NT = (((1,), (1,)), ((), ()))
NN = (((1,), (0,)), ((), ()))
HBM = pl.BlockSpec(memory_space=pltpu.HBM)
VMEM = pl.BlockSpec(memory_space=pltpu.VMEM)


def mm(a, b, dims=NN):
    return lax.dot_general(a, b, dims, preferred_element_type=F32)


def exact(a, b, dims=NN):
    return lax.dot_general(
        a, b, dims, precision=lax.Precision.HIGHEST, preferred_element_type=F32
    )


def params(mib):
    return pltpu.CompilerParams(vmem_limit_bytes=mib * 2**20)


def cost(flops, moved):
    return pl.CostEstimate(flops=flops, bytes_accessed=moved, transcendentals=0)


def paired_coef(v, even_basis, odd_basis):
    zero = jnp.zeros_like(even_basis)
    blocks = jnp.concatenate(
        [
            jnp.concatenate([even_basis, zero], axis=1),
            jnp.concatenate([zero, odd_basis], axis=1),
        ],
        axis=0,
    )
    return mm(v, blocks, NT).astype(BF)


def is_even():
    return (lax.axis_index("leaf") & 1) == 0


def columns_of(start, width):
    return pl.ds(pl.multiple_of(start, width), width)


def split_body(v, va, vb, sems):
    half = va.shape[1]
    start_a = jnp.where(is_even(), half, 0)
    copies = [
        pltpu.make_async_copy(v.at[:, columns_of(start, half)], out, sems.at[i])
        for i, (out, start) in enumerate(((va, start_a), (vb, half - start_a)))
    ]
    for copy in copies:
        copy.start()
    for copy in copies:
        copy.wait()


def split(vectors):
    columns, own = vectors.shape
    return pl.pallas_call(
        split_body,
        in_specs=[HBM],
        out_specs=[VMEM] * 2,
        out_shape=[jax.ShapeDtypeStruct((columns, own // 2), BF)] * 2,
        scratch_shapes=[pltpu.SemaphoreType.DMA((2,))],
        compiler_params=params(4),
        cost_estimate=cost(0, 2_000_000),
        name="split",
    )(pltpu.with_memory_space_constraint(vectors, pltpu.HBM))


def head_body(va, vb, basis_hbm, trans_hbm, coef, node, basis, trans, sems):
    leaves, rank, points = basis.shape
    first_a = jnp.where(is_even(), leaves // 2, 0)
    copies = [
        pltpu.make_async_copy(basis_hbm, basis, sems.at[0]),
        pltpu.make_async_copy(trans_hbm, trans, sems.at[1]),
    ]
    for copy in copies:
        copy.start()
    for copy in copies:
        copy.wait()
    total = None
    for v, first in ((va, first_a), (vb, leaves // 2 - first_a)):
        for pair in range(leaves // 4):
            leaf = first + 2 * pair
            rows = v[:, 2 * pair * points : 2 * (pair + 1) * points]
            both = paired_coef(rows, basis[leaf], basis[leaf + 1])
            at = columns_of((first // 2 + pair) * 2 * rank, 2 * rank)
            coef[:, at] = both
            term = mm(both, trans[at, :])
            total = term if total is None else total + term
    node[...] = total


def head(va, vb, basis_t, trans2):
    columns = va.shape[0]
    leaves, rank, _ = basis_t.shape
    hbm = (pltpu.with_memory_space_constraint(x, pltpu.HBM) for x in (basis_t, trans2))
    return pl.pallas_call(
        head_body,
        in_specs=[VMEM] * 2 + [HBM] * 2,
        out_specs=[VMEM] * 2,
        out_shape=[
            jax.ShapeDtypeStruct((columns, leaves * rank), BF),
            jax.ShapeDtypeStruct((columns, rank), F32),
        ],
        scratch_shapes=[
            pltpu.VMEM(basis_t.shape, BF),
            pltpu.VMEM(trans2.shape, BF),
            pltpu.SemaphoreType.DMA((2,)),
        ],
        compiler_params=params(6),
        cost_estimate=cost(200_000_000, 6_000_000),
        name="head",
    )(va, vb, *hbm)


def load_piece(near, kept, piece, sems):
    some = kept.shape[0] // PIECES
    return [
        pltpu.make_async_copy(near.at[piece * some + i], kept.at[piece * some + i], sems.at[i])
        for i in range(some)
    ]


def table_body(levels, near_list, trans_hbm, couple_hbm, near, up, pair, plan, kept, *scratch):
    trans, couple, sems = scratch
    copies = [
        pltpu.make_async_copy(trans_hbm, trans, sems.at[8]),
        pltpu.make_async_copy(couple_hbm, couple, sems.at[9]),
    ]
    copies += load_piece(near, kept, 0, sems)
    for copy in copies:
        copy.start()
    device = lax.axis_index("leaf")
    kn, leaves = near_list.shape
    first = device * leaves
    even = is_even()

    def scan(leaf, found):
        in_a, in_b = found
        for slot in range(kn):
            source = near_list[slot, leaf] - first
            left = source < 0
            outside = left | (source >= leaves)
            to_a = left != even
            code = (leaf * 8 + slot) * 16 + source + jnp.where(left, REACH, -leaves)
            plan[in_a] = code
            plan[LIST + in_b] = code
            in_a = in_a + jnp.where(outside & to_a, 1, 0)
            in_b = in_b + jnp.where(outside & jnp.logical_not(to_a), 1, 0)
        return in_a, in_b

    found = lax.fori_loop(0, leaves, scan, (jnp.int32(0), jnp.int32(0)))
    for side, total in enumerate(found):
        for i in range(TOGETHER):
            plan[side * LIST + total + i] = (leaves * 8) * 16
        plan[2 * LIST + side] = lax.div(total + TOGETHER - 1, TOGETHER)
    count, rows, nodes = 8, trans.shape[0], trans.shape[2]
    row = lax.broadcasted_iota(jnp.int32, (count, nodes), 0)
    node = lax.broadcasted_iota(jnp.int32, (count, nodes), 1)
    offset = (2 << levels) - lax.shift_right_logical(jnp.full_like(row, 2 << levels), row)
    here = offset + lax.shift_right_logical(jnp.zeros_like(row) + device, row)
    there = jnp.bitwise_xor(here, 1)
    wanted = row < levels
    pick_here = jnp.where(wanted & (node == here), 1.0, 0.0).astype(BF)
    pick_there = jnp.where(wanted & (node == there), 1.0, 0.0).astype(BF)
    both = jnp.concatenate([pick_here, pick_there], axis=0)
    copies[0].wait()
    copies[1].wait()
    for k in range(rows):
        picked = mm(both, trans[k], NT)
        up[0, :, k, :] = picked[:levels]
        up[1, :, k, :] = picked[count : count + levels]
        pair[:, k, :] = mm(pick_here, couple[k], NT)[:levels]
    for copy in copies[2:]:
        copy.wait()


def chain_body(up, pair, down):
    levels = pair.shape[0]
    down[0] = pair[0]
    path = up[0, 0]
    for t in range(1, levels):
        down[t] = exact(path, pair[t])
        if t + 1 < levels:
            path = exact(path, up[0, t])


def chain(up, pair):
    return pl.pallas_call(
        chain_body,
        in_specs=[VMEM] * 2,
        out_specs=VMEM,
        out_shape=jax.ShapeDtypeStruct(pair.shape, F32),
        compiler_params=params(4),
        cost_estimate=cost(10_000_000, 1_000_000),
        name="chain",
    )(up, pair)


def table(top_transfer, top_couple, near_list_t, near_blocks):
    nodes, rank, _ = top_transfer.shape
    levels = lax.axis_size("leaf").bit_length() - 1
    shape = near_blocks.shape
    hbm = (
        jnp.transpose(top_transfer, (1, 2, 0)),
        jnp.transpose(top_couple, (1, 2, 0)),
        near_blocks,
    )
    return pl.pallas_call(
        lambda *refs: table_body(levels, *refs),
        grid_spec=pltpu.PrefetchScalarGridSpec(
            num_scalar_prefetch=1,
            in_specs=[HBM] * 3,
            out_specs=[VMEM, VMEM, pl.BlockSpec(memory_space=pltpu.SMEM), VMEM],
            scratch_shapes=[
                pltpu.VMEM((rank, rank, nodes), BF),
                pltpu.VMEM((rank, rank, nodes), BF),
                pltpu.SemaphoreType.DMA((shape[0] // PIECES + 2,)),
            ],
        ),
        out_shape=[
            jax.ShapeDtypeStruct((2, levels, rank, rank), F32),
            jax.ShapeDtypeStruct((levels, rank, rank), F32),
            jax.ShapeDtypeStruct((2 * LIST + 8,), jnp.int32),
            jax.ShapeDtypeStruct(shape, BF),
        ],
        compiler_params=params(6),
        cost_estimate=cost(10_000_000, 8_000_000),
        name="table",
    )(near_list_t, *(pltpu.with_memory_space_constraint(x, pltpu.HBM) for x in hbm))


def near_body(piece, load, near_list, v, kept, *refs):
    copies = []
    if load:
        near, total, kept, sems = refs
        copies = load_piece(near, kept, piece + 1, sems)
        for copy in copies:
            copy.start()
    else:
        (total,) = refs
    leaves, kn, points, _ = kept.shape
    some = leaves // PIECES
    first = lax.axis_index("leaf") * leaves
    for i in range(some):
        out = None
        leaf = piece * some + i
        for s in range(kn):
            source = near_list[s, leaf] - first
            inside = (source >= 0) & (source < leaves)
            rows = v[:, columns_of(jnp.clip(source, 0, leaves - 1) * points, points)]
            term = mm(jnp.where(inside, rows, jnp.zeros_like(rows)), kept[leaf, s], NT)
            out = term if out is None else out + term
        total[:, i * points : (i + 1) * points] = out
    for copy in copies:
        copy.wait()


def near_piece(piece, near_list_t, v, near_blocks, kept, load):
    columns = v.shape[0]
    leaves, _, points, _ = kept.shape
    some = leaves // PIECES
    in_specs = [VMEM, VMEM]
    args = [v, kept]
    out_shape = [jax.ShapeDtypeStruct((columns, some * points), F32)]
    scratch = []
    if load:
        in_specs.append(HBM)
        args.append(pltpu.with_memory_space_constraint(near_blocks, pltpu.HBM))
        out_shape.append(jax.ShapeDtypeStruct(kept.shape, BF))
        scratch.append(pltpu.SemaphoreType.DMA((some,)))
    return pl.pallas_call(
        lambda *refs: near_body(piece, load, *refs),
        grid_spec=pltpu.PrefetchScalarGridSpec(
            num_scalar_prefetch=1,
            in_specs=in_specs,
            out_specs=[VMEM] * len(out_shape),
            scratch_shapes=scratch,
        ),
        out_shape=out_shape,
        input_output_aliases={2: 1} if load else {},
        compiler_params=params(4),
        cost_estimate=cost(350_000_000, 6_000_000),
    )(near_list_t, *args)


def add_halo(side, plan, v, near, acc):
    leaves, _, points, _ = near.shape

    def add(j, carry):
        terms = []
        for i in range(TOGETHER):
            code = plan[side * LIST + j * TOGETHER + i]
            leaf = lax.shift_right_logical(code, 7)
            slot = lax.shift_right_logical(code, 4) & 7
            rows = v[:, columns_of((code & 15) * points, points)]
            term = mm(rows, near[leaf & (leaves - 1), slot], NT)
            terms.append((columns_of(leaf * points, points), term))
        for here, term in terms:
            acc[:, here] += term
        return carry

    lax.fori_loop(0, plan[2 * LIST + side], add, 0)


def unpack(coef, base, table_ref):
    wide = table_ref.shape[2]
    row = lax.broadcasted_iota(jnp.int32, (wide, wide), 0)
    lane = lax.broadcasted_iota(jnp.int32, (wide, wide), 1)
    swap = jnp.where(jnp.bitwise_xor(row, wide // 2) == lane, 1.0, 0.0).astype(BF)
    for pair in range(coef.shape[1] // wide):
        both = coef[:, wide * pair : wide * (pair + 1)]
        table_ref[base + 2 * pair] = both
        table_ref[base + 2 * pair + 1] = mm(both, swap).astype(BF)


def side_body(plan, got_va, got_ca, sent_c, near, *refs):
    partial, (acc, table_ref) = refs[:PIECES], refs[PIECES:]
    leaves = near.shape[0]
    for piece, part in enumerate(partial):
        width = part.shape[1]
        acc[:, piece * width : (piece + 1) * width] = part[...]
    unpack(sent_c, leaves, table_ref)
    unpack(got_ca, jnp.where(is_even(), 2 * leaves, 0), table_ref)
    add_halo(0, plan, got_va, near, acc)


def side_a(plan, got_va, got_ca, sent_c, kept, partial):
    columns = sent_c.shape[0]
    leaves, _, points, _ = kept.shape
    rank = sent_c.shape[1] // leaves
    return pl.pallas_call(
        side_body,
        grid_spec=pltpu.PrefetchScalarGridSpec(
            num_scalar_prefetch=1,
            in_specs=[VMEM] * (4 + PIECES),
            out_specs=[VMEM] * 2,
        ),
        out_shape=[
            jax.ShapeDtypeStruct((columns, (leaves + 1) * points), F32),
            jax.ShapeDtypeStruct((3 * leaves, columns, 2 * rank), BF),
        ],
        compiler_params=params(4),
        cost_estimate=cost(400_000_000, 6_000_000),
        name="side",
    )(plan, got_va, got_ca, sent_c, kept, *partial)


def tail_body(names, sides, more, *refs):
    r = dict(zip(names, refs))
    acc, table_ref, couple_list = r["acc"], r["table"], r["couple_list"]
    basis, trans, couple, image = r["basis"], r["trans"], r["couple"], r["image"]
    leaves, rank, points = basis.shape
    group = leaves // 4
    even = is_even()
    first = lax.axis_index("leaf") * leaves
    first_b = jnp.where(even, 0, leaves // 2)
    descent = r["top"][...].astype(BF)
    if "b" in sides:
        unpack(r["got_cb"], jnp.where(even, 0, 2 * leaves), table_ref)
        add_halo(1, r["plan"], r["got_vb"], r["near"], acc)
    own_v = r["own_v"]
    writes = []
    total = r["node_in"][...] if "node_in" in r else None
    for side in sides:
        start = first_b if side == "b" else leaves // 2 - first_b
        for part in range(2):
            base = start + part * group
            results = []
            for i in range(group):
                leaf = base + i
                moved = trans[columns_of(leaf * rank, rank), :]
                local = mm(descent, moved, NT)
                for s in range(couple.shape[1]):
                    source = couple_list[s, leaf] - first + FARR
                    local += mm(table_ref[source, :, :rank], couple[leaf, s], NT)
                here = columns_of(leaf * points, points)
                value = (acc[:, here] + mm(local.astype(BF), basis[leaf])).astype(BF)
                results.append(value)
                own_v[:, here] = value
                if more:
                    at = (part * group + i) * points
                    r["message"][:, at : at + points] = value
            here = columns_of(base * points, group * points)
            writes.append(
                pltpu.make_async_copy(own_v.at[:, here], image.at[:, here], r["sems"].at[len(writes)])
            )
            writes[-1].start()
            if not more:
                continue
            for pair in range(group // 2):
                leaf = base + 2 * pair
                rows = jnp.concatenate(results[2 * pair : 2 * pair + 2], axis=1)
                both = paired_coef(rows, basis[leaf], basis[leaf + 1])
                at = columns_of((base // 2 + pair) * 2 * rank, 2 * rank)
                r["coef"][:, at] = both
                term = mm(both, trans[at, :])
                total = term if total is None else total + term
    if more:
        r["node"][...] = total
    for write in writes:
        write.wait()


def tail(sides, more, scalars, inputs, carried):
    leaves, rank, points = inputs["basis"].shape
    columns = inputs["top"].shape[0]
    own = leaves * points
    fresh = {}
    if "image" not in carried:
        fresh["image"] = jax.ShapeDtypeStruct((columns, own), BF)
    if more:
        if "own_v" not in carried:
            fresh["own_v"] = jax.ShapeDtypeStruct((columns, own), BF)
            fresh["coef"] = jax.ShapeDtypeStruct((columns, leaves * rank), BF)
        fresh["message"] = jax.ShapeDtypeStruct((columns, own // 2), BF)
        fresh["node"] = jax.ShapeDtypeStruct((columns, rank), F32)
    outs = [*carried, *fresh]
    before = [*scalars, *inputs]
    names = [*before, *(f"old_{name}" for name in carried), *outs]
    scratch = [pltpu.SemaphoreType.DMA((4,))]
    names.append("sems")
    if not more:
        scratch.append(pltpu.VMEM((columns, own), BF))
        names.append("own_v")
    spec = lambda name: HBM if name == "image" else VMEM
    result = pl.pallas_call(
        lambda *refs: tail_body(names, sides, more, *refs),
        grid_spec=pltpu.PrefetchScalarGridSpec(
            num_scalar_prefetch=len(scalars),
            in_specs=[VMEM] * len(inputs) + [spec(name) for name in carried],
            out_specs=[spec(name) for name in outs],
            scratch_shapes=scratch,
        ),
        out_shape=[
            jax.ShapeDtypeStruct(carried[name].shape, carried[name].dtype)
            if name in carried
            else fresh[name]
            for name in outs
        ],
        input_output_aliases={len(before) + i: i for i in range(len(carried))},
        compiler_params=params(6),
        cost_estimate=cost(600_000_000, 6_000_000),
    )(*scalars.values(), *inputs.values(), *carried.values())
    return dict(zip(outs, result))


def swapped(value, mask):
    return lax.ppermute(value, "leaf", [(i, i ^ mask) for i in range(lax.axis_size("leaf"))])


def swapped_odd(value):
    size = lax.axis_size("leaf")
    pairs = [(i, i + 1) for i in range(1, size - 1, 2)]
    return lax.ppermute(value, "leaf", pairs + [(j, i) for i, j in pairs])


def one_product(node, va, coef, got_va, fill, tables):
    levels = lax.axis_size("leaf").bit_length() - 1
    top = jnp.zeros_like(node)
    got_ca = got_cb = None
    others = []
    for t in range(levels):
        mask = (1 << t) if t % 2 == 0 else 3 << (t - 1)
        other = swapped(node, mask)
        fill(t)
        up, down = tables(t)
        if t == 0:
            if got_va is None:
                got_va = swapped(va, 1)
            got_ca = swapped(coef, 1)
            got_cb = swapped_odd(coef)
        if t + 1 < levels:
            node = exact(node, up[0, t]) + exact(other, up[1, t])
        others.append(other)
    for t, other in enumerate(others):
        top += exact(other, down[t], NT)
    return top, got_va, got_ca, got_cb


def on_device(
    rhs_block,
    basis_t,
    near_blocks,
    near_list,
    leaf_transfer,
    couple_list,
    leaf_couple,
    top_transfer,
    top_couple,
):
    leaves, rank, _ = leaf_transfer.shape
    trans2 = leaf_transfer.reshape(leaves * rank, rank)
    near_list_t, couple_list_t = near_list.T, couple_list.T
    made = {}
    partial, again = [], []

    def fill_first(t):
        if t == 0:
            made["up"], made["pair"], made["plan"], made["kept"] = table(
                top_transfer, top_couple, near_list_t, near_blocks
            )
        elif t <= PIECES:
            load = t < PIECES
            out = near_piece(t - 1, near_list_t, rhs_block, near_blocks, made["kept"], load)
            partial.append(out[0])
            if load:
                made["kept"] = out[1]

    def tables(t):
        if t == 4 and "down" not in made:
            made["down"] = chain(made["up"], made["pair"])
        return made["up"], made.get("down")

    def fill_second(t):
        for piece in {1: (0, 1), 2: (2,), 3: (3,)}.get(t, ()):
            (out,) = near_piece(piece, near_list_t, made["own_v"], near_blocks, made["kept"], False)
            again.append(out)

    def parts(top, got_vb, got_cb):
        scalars = {"plan": made["plan"], "couple_list": couple_list_t}
        inputs = {"top": top, "basis": basis_t, "trans": trans2, "couple": leaf_couple}
        on_b = {"got_vb": got_vb, "got_cb": got_cb, "near": made["kept"]}
        return scalars, inputs, on_b

    va, vb = split(rhs_block)
    got_va = swapped(va, 1)
    got_vb = swapped_odd(vb)
    coef, node = head(va, vb, basis_t, trans2)
    top, _, got_ca, got_cb = one_product(node, va, coef, got_va, fill_first, tables)
    acc, entries = side_a(made["plan"], got_va, got_ca, coef, made["kept"], partial)
    scalars, inputs, on_b = parts(top, got_vb, got_cb)
    half = tail("b", True, scalars, {**inputs, **on_b}, {"acc": acc, "table": entries})
    got_vb = swapped_odd(half["message"])
    inputs["node_in"] = half["node"]
    carried = {k: half[k] for k in ("acc", "table", "image", "own_v", "coef")}
    rest = tail("a", True, scalars, inputs, carried)
    first_image, coef, made["own_v"] = rest["image"], rest["coef"], rest["own_v"]
    top, got_va, got_ca, got_cb = one_product(
        rest["node"], rest["message"], coef, None, fill_second, tables
    )
    acc, entries = side_a(made["plan"], got_va, got_ca, coef, made["kept"], again)
    scalars, inputs, on_b = parts(top, got_vb, got_cb)
    last = tail("ba", False, scalars, {**inputs, **on_b}, {"acc": acc, "table": entries})
    return (first_image, last["image"])


def solution(mesh):
    in_specs = (
        P("rhs", "leaf"),
        P("leaf", None, None),
        P("leaf", None, None, None),
        P("leaf", None),
        P("leaf", None, None),
        P("leaf", None),
        P("leaf", None, None, None),
        P(),
        P(),
    )
    out_specs = (P("rhs", "leaf"), P("rhs", "leaf"))
    return jax.shard_map(
        on_device, mesh=mesh, in_specs=in_specs, out_specs=out_specs, check_vma=False
    )
```

```python
import jax
import jax.numpy as jnp
from jax import lax
from jax.experimental import pallas as pl
from jax.experimental.pallas import tpu as pltpu
from jax.sharding import PartitionSpec as P


REACH = 16
FARR = 32
PIECES = 4
TOGETHER = 8
LIST = 80
BF = jnp.bfloat16
F32 = jnp.float32
NT = (((1,), (1,)), ((), ()))
NN = (((1,), (0,)), ((), ()))
HBM = pl.BlockSpec(memory_space=pltpu.HBM)
VMEM = pl.BlockSpec(memory_space=pltpu.VMEM)


def mm(a, b, dims=NN):
    return lax.dot_general(a, b, dims, preferred_element_type=F32)


def exact(a, b, dims=NN):
    return lax.dot_general(
        a, b, dims, precision=lax.Precision.HIGHEST, preferred_element_type=F32
    )


def params(mib):
    return pltpu.CompilerParams(vmem_limit_bytes=mib * 2**20)


def cost(flops, moved):
    return pl.CostEstimate(flops=flops, bytes_accessed=moved, transcendentals=0)


def paired_coef(v, even_basis, odd_basis):
    zero = jnp.zeros_like(even_basis)
    blocks = jnp.concatenate(
        [
            jnp.concatenate([even_basis, zero], axis=1),
            jnp.concatenate([zero, odd_basis], axis=1),
        ],
        axis=0,
    )
    return mm(v, blocks, NT).astype(BF)


def is_even():
    return (lax.axis_index("leaf") & 1) == 0


def columns_of(start, width):
    return pl.ds(pl.multiple_of(start, width), width)


def load_piece(near, kept, piece, sems, at=0):
    some = kept.shape[0] // PIECES
    return [
        pltpu.make_async_copy(near.at[piece * some + i], kept.at[piece * some + i], sems.at[at + i])
        for i in range(some)
    ]


def split_body(v, va, vb, sems):
    half = va.shape[1]
    start_a = jnp.where(is_even(), half, 0)
    copies = [
        pltpu.make_async_copy(v.at[:, columns_of(start, half)], out, sems.at[i])
        for i, (out, start) in enumerate(((va, start_a), (vb, half - start_a)))
    ]
    for copy in copies:
        copy.start()
    for copy in copies:
        copy.wait()


def split(vectors):
    columns, own = vectors.shape
    return pl.pallas_call(
        split_body,
        in_specs=[HBM],
        out_specs=[VMEM] * 2,
        out_shape=[jax.ShapeDtypeStruct((columns, own // 2), BF)] * 2,
        scratch_shapes=[pltpu.SemaphoreType.DMA((2,))],
        compiler_params=params(4),
        cost_estimate=cost(0, 2_000_000),
        name="split",
    )(pltpu.with_memory_space_constraint(vectors, pltpu.HBM))


def head_body(va, vb, basis_hbm, trans_hbm, near, coef, node, kept, basis, trans, sems):
    leaves, rank, points = basis.shape
    first_a = jnp.where(is_even(), leaves // 2, 0)
    copies = [
        pltpu.make_async_copy(basis_hbm, basis, sems.at[0]),
        pltpu.make_async_copy(trans_hbm, trans, sems.at[1]),
    ]
    later = load_piece(near, kept, 0, sems, 2)
    for copy in copies + later:
        copy.start()
    for copy in copies:
        copy.wait()
    total = None
    for v, first in ((va, first_a), (vb, leaves // 2 - first_a)):
        for pair in range(leaves // 4):
            leaf = first + 2 * pair
            rows = v[:, 2 * pair * points : 2 * (pair + 1) * points]
            both = paired_coef(rows, basis[leaf], basis[leaf + 1])
            at = columns_of((first // 2 + pair) * 2 * rank, 2 * rank)
            coef[:, at] = both
            term = mm(both, trans[at, :])
            total = term if total is None else total + term
    node[...] = total
    for copy in later:
        copy.wait()


def head(va, vb, basis_t, trans2, near_blocks):
    columns = va.shape[0]
    leaves, rank, _ = basis_t.shape
    arrays = (basis_t, trans2, near_blocks)
    hbm = (pltpu.with_memory_space_constraint(x, pltpu.HBM) for x in arrays)
    return pl.pallas_call(
        head_body,
        in_specs=[VMEM] * 2 + [HBM] * 3,
        out_specs=[VMEM] * 3,
        out_shape=[
            jax.ShapeDtypeStruct((columns, leaves * rank), BF),
            jax.ShapeDtypeStruct((columns, rank), F32),
            jax.ShapeDtypeStruct(near_blocks.shape, BF),
        ],
        scratch_shapes=[
            pltpu.VMEM(basis_t.shape, BF),
            pltpu.VMEM(trans2.shape, BF),
            pltpu.SemaphoreType.DMA((2 + leaves // PIECES,)),
        ],
        compiler_params=params(6),
        cost_estimate=cost(200_000_000, 6_000_000),
        name="head",
    )(va, vb, *hbm)


def table_body(
    levels, near_list, trans_hbm, couple_hbm, near, old_kept, up, pair, plan, kept, *scratch
):
    trans, couple, sems = scratch
    copies = [
        pltpu.make_async_copy(trans_hbm, trans, sems.at[0]),
        pltpu.make_async_copy(couple_hbm, couple, sems.at[1]),
    ]
    copies += load_piece(near, kept, 1, sems, 2)
    copies += load_piece(near, kept, 2, sems, len(copies))
    for copy in copies:
        copy.start()
    device = lax.axis_index("leaf")
    kn, leaves = near_list.shape
    first = device * leaves
    even = is_even()

    def scan(leaf, found):
        in_a, in_b = found
        for slot in range(kn):
            source = near_list[slot, leaf] - first
            left = source < 0
            outside = left | (source >= leaves)
            to_a = left != even
            code = (leaf * 8 + slot) * 16 + source + jnp.where(left, REACH, -leaves)
            plan[in_a] = code
            plan[LIST + in_b] = code
            in_a = in_a + jnp.where(outside & to_a, 1, 0)
            in_b = in_b + jnp.where(outside & jnp.logical_not(to_a), 1, 0)
        return in_a, in_b

    found = lax.fori_loop(0, leaves, scan, (jnp.int32(0), jnp.int32(0)))
    for side, total in enumerate(found):
        for i in range(TOGETHER):
            plan[side * LIST + total + i] = (leaves * 8) * 16
        plan[2 * LIST + side] = lax.div(total + TOGETHER - 1, TOGETHER)
    count, rows, nodes = 8, trans.shape[0], trans.shape[2]
    row = lax.broadcasted_iota(jnp.int32, (count, nodes), 0)
    node = lax.broadcasted_iota(jnp.int32, (count, nodes), 1)
    offset = (2 << levels) - lax.shift_right_logical(jnp.full_like(row, 2 << levels), row)
    here = offset + lax.shift_right_logical(jnp.zeros_like(row) + device, row)
    there = jnp.bitwise_xor(here, 1)
    wanted = row < levels
    pick_here = jnp.where(wanted & (node == here), 1.0, 0.0).astype(BF)
    pick_there = jnp.where(wanted & (node == there), 1.0, 0.0).astype(BF)
    both = jnp.concatenate([pick_here, pick_there], axis=0)
    copies[0].wait()
    copies[1].wait()
    for k in range(rows):
        picked = mm(both, trans[k], NT)
        up[0, :, k, :] = picked[:levels]
        up[1, :, k, :] = picked[count : count + levels]
        pair[:, k, :] = mm(pick_here, couple[k], NT)[:levels]
    for copy in copies[2:]:
        copy.wait()


def chain_body(up, pair, down):
    levels = pair.shape[0]
    down[0] = pair[0]
    path = up[0, 0]
    for t in range(1, levels):
        down[t] = exact(path, pair[t])
        if t + 1 < levels:
            path = exact(path, up[0, t])


def chain(up, pair):
    return pl.pallas_call(
        chain_body,
        in_specs=[VMEM] * 2,
        out_specs=VMEM,
        out_shape=jax.ShapeDtypeStruct(pair.shape, F32),
        compiler_params=params(4),
        cost_estimate=cost(10_000_000, 1_000_000),
        name="chain",
    )(up, pair)


def table(top_transfer, top_couple, near_list_t, near_blocks, kept):
    nodes, rank, _ = top_transfer.shape
    levels = lax.axis_size("leaf").bit_length() - 1
    shape = near_blocks.shape
    hbm = (
        jnp.transpose(top_transfer, (1, 2, 0)),
        jnp.transpose(top_couple, (1, 2, 0)),
        near_blocks,
    )
    return pl.pallas_call(
        lambda *refs: table_body(levels, *refs),
        grid_spec=pltpu.PrefetchScalarGridSpec(
            num_scalar_prefetch=1,
            in_specs=[HBM] * 3 + [VMEM],
            out_specs=[VMEM, VMEM, pl.BlockSpec(memory_space=pltpu.SMEM), VMEM],
            scratch_shapes=[
                pltpu.VMEM((rank, rank, nodes), BF),
                pltpu.VMEM((rank, rank, nodes), BF),
                pltpu.SemaphoreType.DMA((2 * (shape[0] // PIECES) + 2,)),
            ],
        ),
        out_shape=[
            jax.ShapeDtypeStruct((2, levels, rank, rank), F32),
            jax.ShapeDtypeStruct((levels, rank, rank), F32),
            jax.ShapeDtypeStruct((2 * LIST + 8,), jnp.int32),
            jax.ShapeDtypeStruct(shape, BF),
        ],
        input_output_aliases={4: 3},
        compiler_params=params(6),
        cost_estimate=cost(10_000_000, 8_000_000),
        name="table",
    )(near_list_t, *(pltpu.with_memory_space_constraint(x, pltpu.HBM) for x in hbm), kept)


def near_body(piece, load, near_list, v, kept, *refs):
    copies = []
    if load:
        near, total, kept, sems = refs
        copies = load_piece(near, kept, PIECES - 1, sems)
        for copy in copies:
            copy.start()
    else:
        (total,) = refs
    leaves, kn, points, _ = kept.shape
    some = leaves // PIECES
    first = lax.axis_index("leaf") * leaves
    for i in range(some):
        out = None
        leaf = piece * some + i
        for s in range(kn):
            source = near_list[s, leaf] - first
            inside = (source >= 0) & (source < leaves)
            rows = v[:, columns_of(jnp.clip(source, 0, leaves - 1) * points, points)]
            term = mm(jnp.where(inside, rows, jnp.zeros_like(rows)), kept[leaf, s], NT)
            out = term if out is None else out + term
        total[:, i * points : (i + 1) * points] = out
    for copy in copies:
        copy.wait()


def near_piece(piece, near_list_t, v, near_blocks, kept, load):
    columns = v.shape[0]
    leaves, _, points, _ = kept.shape
    some = leaves // PIECES
    in_specs = [VMEM, VMEM]
    args = [v, kept]
    out_shape = [jax.ShapeDtypeStruct((columns, some * points), F32)]
    scratch = []
    if load:
        in_specs.append(HBM)
        args.append(pltpu.with_memory_space_constraint(near_blocks, pltpu.HBM))
        out_shape.append(jax.ShapeDtypeStruct(kept.shape, BF))
        scratch.append(pltpu.SemaphoreType.DMA((some,)))
    return pl.pallas_call(
        lambda *refs: near_body(piece, load, *refs),
        grid_spec=pltpu.PrefetchScalarGridSpec(
            num_scalar_prefetch=1,
            in_specs=in_specs,
            out_specs=[VMEM] * len(out_shape),
            scratch_shapes=scratch,
        ),
        out_shape=out_shape,
        input_output_aliases={2: 1} if load else {},
        compiler_params=params(4),
        cost_estimate=cost(350_000_000, 6_000_000),
    )(near_list_t, *args)


def add_halo(side, plan, v, near, acc):
    leaves, _, points, _ = near.shape

    def add(j, carry):
        terms = []
        for i in range(TOGETHER):
            code = plan[side * LIST + j * TOGETHER + i]
            leaf = lax.shift_right_logical(code, 7)
            slot = lax.shift_right_logical(code, 4) & 7
            rows = v[:, columns_of((code & 15) * points, points)]
            term = mm(rows, near[leaf & (leaves - 1), slot], NT)
            terms.append((columns_of(leaf * points, points), term))
        for here, term in terms:
            acc[:, here] += term
        return carry

    lax.fori_loop(0, plan[2 * LIST + side], add, 0)


def unpack(coef, base, table_ref):
    wide = table_ref.shape[2]
    row = lax.broadcasted_iota(jnp.int32, (wide, wide), 0)
    lane = lax.broadcasted_iota(jnp.int32, (wide, wide), 1)
    swap = jnp.where(jnp.bitwise_xor(row, wide // 2) == lane, 1.0, 0.0).astype(BF)
    for pair in range(coef.shape[1] // wide):
        both = coef[:, wide * pair : wide * (pair + 1)]
        table_ref[base + 2 * pair] = both
        table_ref[base + 2 * pair + 1] = mm(both, swap).astype(BF)


def side_body(plan, got_va, got_ca, sent_c, near, *refs):
    partial, (acc, table_ref) = refs[:PIECES], refs[PIECES:]
    leaves = near.shape[0]
    for piece, part in enumerate(partial):
        width = part.shape[1]
        acc[:, piece * width : (piece + 1) * width] = part[...]
    unpack(sent_c, leaves, table_ref)
    unpack(got_ca, jnp.where(is_even(), 2 * leaves, 0), table_ref)
    add_halo(0, plan, got_va, near, acc)


def side_a(plan, got_va, got_ca, sent_c, kept, partial):
    columns = sent_c.shape[0]
    leaves, _, points, _ = kept.shape
    rank = sent_c.shape[1] // leaves
    return pl.pallas_call(
        side_body,
        grid_spec=pltpu.PrefetchScalarGridSpec(
            num_scalar_prefetch=1,
            in_specs=[VMEM] * (4 + PIECES),
            out_specs=[VMEM] * 2,
        ),
        out_shape=[
            jax.ShapeDtypeStruct((columns, (leaves + 1) * points), F32),
            jax.ShapeDtypeStruct((3 * leaves, columns, 2 * rank), BF),
        ],
        compiler_params=params(4),
        cost_estimate=cost(400_000_000, 6_000_000),
        name="side",
    )(plan, got_va, got_ca, sent_c, kept, *partial)


def side_b_body(plan, got_vb, got_cb, near, old_acc, old_table, acc, table_ref):
    leaves = near.shape[0]
    unpack(got_cb, jnp.where(is_even(), 0, 2 * leaves), table_ref)
    add_halo(1, plan, got_vb, near, acc)


def side_b(plan, got_vb, got_cb, kept, acc, entries):
    return pl.pallas_call(
        side_b_body,
        grid_spec=pltpu.PrefetchScalarGridSpec(
            num_scalar_prefetch=1,
            in_specs=[VMEM] * 5,
            out_specs=[VMEM] * 2,
        ),
        out_shape=[
            jax.ShapeDtypeStruct(acc.shape, acc.dtype),
            jax.ShapeDtypeStruct(entries.shape, entries.dtype),
        ],
        input_output_aliases={4: 0, 5: 1},
        compiler_params=params(4),
        cost_estimate=cost(200_000_000, 3_000_000),
        name="side_b",
    )(plan, got_vb, got_cb, kept, acc, entries)


def tail_body(names, sides, more, *refs):
    r = dict(zip(names, refs))
    acc, table_ref, couple_list = r["acc"], r["table"], r["couple_list"]
    basis, trans, couple, image = r["basis"], r["trans"], r["couple"], r["image"]
    leaves, rank, points = basis.shape
    group = leaves // 4
    even = is_even()
    first = lax.axis_index("leaf") * leaves
    first_b = jnp.where(even, 0, leaves // 2)
    descent = r["top"][...].astype(BF)
    own_v = r["own_v"]
    writes = []
    total = r["node_in"][...] if "node_in" in r else None
    for side in sides:
        start = first_b if side == "b" else leaves // 2 - first_b
        for part in range(2):
            base = start + part * group
            results = []
            for i in range(group):
                leaf = base + i
                moved = trans[columns_of(leaf * rank, rank), :]
                local = mm(descent, moved, NT)
                for s in range(couple.shape[1]):
                    source = couple_list[s, leaf] - first + FARR
                    local += mm(table_ref[source, :, :rank], couple[leaf, s], NT)
                here = columns_of(leaf * points, points)
                value = (acc[:, here] + mm(local.astype(BF), basis[leaf])).astype(BF)
                results.append(value)
                own_v[:, here] = value
                if more:
                    at = (part * group + i) * points
                    r["message"][:, at : at + points] = value
            here = columns_of(base * points, group * points)
            writes.append(
                pltpu.make_async_copy(own_v.at[:, here], image.at[:, here], r["sems"].at[len(writes)])
            )
            writes[-1].start()
            if not more:
                continue
            for pair in range(group // 2):
                leaf = base + 2 * pair
                rows = jnp.concatenate(results[2 * pair : 2 * pair + 2], axis=1)
                both = paired_coef(rows, basis[leaf], basis[leaf + 1])
                at = columns_of((base // 2 + pair) * 2 * rank, 2 * rank)
                r["coef"][:, at] = both
                term = mm(both, trans[at, :])
                total = term if total is None else total + term
    if more:
        r["node"][...] = total
    for write in writes:
        write.wait()


def tail(sides, more, scalars, inputs, carried):
    leaves, rank, points = inputs["basis"].shape
    columns = inputs["top"].shape[0]
    own = leaves * points
    fresh = {}
    if "image" not in carried:
        fresh["image"] = jax.ShapeDtypeStruct((columns, own), BF)
    if more:
        if "own_v" not in carried:
            fresh["own_v"] = jax.ShapeDtypeStruct((columns, own), BF)
            fresh["coef"] = jax.ShapeDtypeStruct((columns, leaves * rank), BF)
        fresh["message"] = jax.ShapeDtypeStruct((columns, own // 2), BF)
        fresh["node"] = jax.ShapeDtypeStruct((columns, rank), F32)
    outs = [*carried, *fresh]
    before = [*scalars, *inputs]
    names = [*before, *(f"old_{name}" for name in carried), *outs]
    scratch = [pltpu.SemaphoreType.DMA((4,))]
    names.append("sems")
    if not more:
        scratch.append(pltpu.VMEM((columns, own), BF))
        names.append("own_v")
    spec = lambda name: HBM if name == "image" else VMEM
    result = pl.pallas_call(
        lambda *refs: tail_body(names, sides, more, *refs),
        grid_spec=pltpu.PrefetchScalarGridSpec(
            num_scalar_prefetch=len(scalars),
            in_specs=[VMEM] * len(inputs) + [spec(name) for name in carried],
            out_specs=[spec(name) for name in outs],
            scratch_shapes=scratch,
        ),
        out_shape=[
            jax.ShapeDtypeStruct(carried[name].shape, carried[name].dtype)
            if name in carried
            else fresh[name]
            for name in outs
        ],
        input_output_aliases={len(before) + i: i for i in range(len(carried))},
        compiler_params=params(6),
        cost_estimate=cost(600_000_000, 6_000_000),
    )(*scalars.values(), *inputs.values(), *carried.values())
    return dict(zip(outs, result))


def swapped(value, mask):
    return lax.ppermute(value, "leaf", [(i, i ^ mask) for i in range(lax.axis_size("leaf"))])


def swapped_odd(value):
    size = lax.axis_size("leaf")
    pairs = [(i, i + 1) for i in range(1, size - 1, 2)]
    return lax.ppermute(value, "leaf", pairs + [(j, i) for i, j in pairs])


def one_product(node, va, coef, got_va, fill, tables):
    levels = lax.axis_size("leaf").bit_length() - 1
    top = jnp.zeros_like(node)
    got_ca = got_cb = None
    others = []
    for t in range(levels):
        mask = (1 << t) if t % 2 == 0 else 3 << (t - 1)
        other = swapped(node, mask)
        fill(t)
        up, down = tables(t)
        if t == 0:
            if got_va is None:
                got_va = swapped(va, 1)
            got_ca = swapped(coef, 1)
            got_cb = swapped_odd(coef)
        if t + 1 < levels:
            node = exact(node, up[0, t]) + exact(other, up[1, t])
        others.append(other)
    for t, other in enumerate(others):
        top += exact(other, down[t], NT)
    return top, got_va, got_ca, got_cb


def on_device(
    rhs_block,
    basis_t,
    near_blocks,
    near_list,
    leaf_transfer,
    couple_list,
    leaf_couple,
    top_transfer,
    top_couple,
):
    leaves, rank, _ = leaf_transfer.shape
    trans2 = leaf_transfer.reshape(leaves * rank, rank)
    near_list_t, couple_list_t = near_list.T, couple_list.T
    made = {}
    partial, again = [], []

    def fill_first(t):
        if t == 0:
            made["up"], made["pair"], made["plan"], made["kept"] = table(
                top_transfer, top_couple, near_list_t, near_blocks, made["kept"]
            )
        elif t <= PIECES:
            load = t == 1
            out = near_piece(t - 1, near_list_t, rhs_block, near_blocks, made["kept"], load)
            partial.append(out[0])
            if load:
                made["kept"] = out[1]

    def tables(t):
        if t == 4 and "down" not in made:
            made["down"] = chain(made["up"], made["pair"])
        return made["up"], made.get("down")

    def fill_second(t):
        for piece in {1: (0, 1), 2: (2,), 3: (3,)}.get(t, ()):
            (out,) = near_piece(piece, near_list_t, made["own_v"], near_blocks, made["kept"], False)
            again.append(out)

    scalars = {"couple_list": couple_list_t}

    def parts(top):
        return {"top": top, "basis": basis_t, "trans": trans2, "couple": leaf_couple}

    def sides(got_va, got_vb, got_ca, got_cb, coef, own):
        acc, entries = side_a(made["plan"], got_va, got_ca, coef, made["kept"], own)
        acc, entries = side_b(made["plan"], got_vb, got_cb, made["kept"], acc, entries)
        return {"acc": acc, "table": entries}

    va, vb = split(rhs_block)
    got_va = swapped(va, 1)
    got_vb = swapped_odd(vb)
    coef, node, made["kept"] = head(va, vb, basis_t, trans2, near_blocks)
    top, _, got_ca, got_cb = one_product(node, va, coef, got_va, fill_first, tables)
    carried = sides(got_va, got_vb, got_ca, got_cb, coef, partial)
    inputs = parts(top)
    half = tail("b", True, scalars, inputs, carried)
    got_vb = swapped_odd(half["message"])
    inputs = {**inputs, "node_in": half["node"]}
    carried = {k: half[k] for k in ("acc", "table", "image", "own_v", "coef")}
    rest = tail("a", True, scalars, inputs, carried)
    first_image, coef, made["own_v"] = rest["image"], rest["coef"], rest["own_v"]
    top, got_va, got_ca, got_cb = one_product(
        rest["node"], rest["message"], coef, None, fill_second, tables
    )
    carried = sides(got_va, got_vb, got_ca, got_cb, coef, again)
    last = tail("ba", False, scalars, parts(top), carried)
    return (first_image, last["image"])


def solution(mesh):
    in_specs = (
        P("rhs", "leaf"),
        P("leaf", None, None),
        P("leaf", None, None, None),
        P("leaf", None),
        P("leaf", None, None),
        P("leaf", None),
        P("leaf", None, None, None),
        P(),
        P(),
    )
    out_specs = (P("rhs", "leaf"), P("rhs", "leaf"))
    return jax.shard_map(
        on_device, mesh=mesh, in_specs=in_specs, out_specs=out_specs, check_vma=False
    )
```

```python
import jax
import jax.numpy as jnp
from jax import lax
from jax.experimental import pallas as pl
from jax.experimental.pallas import tpu as pltpu
from jax.sharding import PartitionSpec as P


REACH = 16
FARR = 32
PIECES = 4
TOGETHER = 8
LIST = 80
BF = jnp.bfloat16
F32 = jnp.float32
NT = (((1,), (1,)), ((), ()))
NN = (((1,), (0,)), ((), ()))
HBM = pl.BlockSpec(memory_space=pltpu.HBM)
VMEM = pl.BlockSpec(memory_space=pltpu.VMEM)


def mm(a, b, dims=NN):
    return lax.dot_general(a, b, dims, preferred_element_type=F32)


def exact(a, b, dims=NN):
    return lax.dot_general(
        a, b, dims, precision=lax.Precision.HIGHEST, preferred_element_type=F32
    )


def params(mib):
    return pltpu.CompilerParams(vmem_limit_bytes=mib * 2**20)


def cost(flops, moved):
    return pl.CostEstimate(flops=flops, bytes_accessed=moved, transcendentals=0)


def paired_coef(v, even_basis, odd_basis):
    zero = jnp.zeros_like(even_basis)
    blocks = jnp.concatenate(
        [
            jnp.concatenate([even_basis, zero], axis=1),
            jnp.concatenate([zero, odd_basis], axis=1),
        ],
        axis=0,
    )
    return mm(v, blocks, NT).astype(BF)


def is_even():
    return (lax.axis_index("leaf") & 1) == 0


def columns_of(start, width):
    return pl.ds(pl.multiple_of(start, width), width)


def load_piece(near, kept, piece, sems, at=0):
    some = kept.shape[0] // PIECES
    return [
        pltpu.make_async_copy(near.at[piece * some + i], kept.at[piece * some + i], sems.at[at + i])
        for i in range(some)
    ]


def split_body(v, va, vb, sems):
    half = va.shape[1]
    start_a = jnp.where(is_even(), half, 0)
    copies = [
        pltpu.make_async_copy(v.at[:, columns_of(start, half)], out, sems.at[i])
        for i, (out, start) in enumerate(((va, start_a), (vb, half - start_a)))
    ]
    for copy in copies:
        copy.start()
    for copy in copies:
        copy.wait()


def split(vectors):
    columns, own = vectors.shape
    return pl.pallas_call(
        split_body,
        in_specs=[HBM],
        out_specs=[VMEM] * 2,
        out_shape=[jax.ShapeDtypeStruct((columns, own // 2), BF)] * 2,
        scratch_shapes=[pltpu.SemaphoreType.DMA((2,))],
        compiler_params=params(4),
        cost_estimate=cost(0, 2_000_000),
        name="split",
    )(pltpu.with_memory_space_constraint(vectors, pltpu.HBM))


def head_body(va, vb, basis_hbm, trans_hbm, near, coef, node, kept, basis, trans, sems):
    leaves, rank, points = basis.shape
    first_a = jnp.where(is_even(), leaves // 2, 0)
    copies = [
        pltpu.make_async_copy(basis_hbm, basis, sems.at[0]),
        pltpu.make_async_copy(trans_hbm, trans, sems.at[1]),
    ]
    later = load_piece(near, kept, 0, sems, 2)
    for copy in copies + later:
        copy.start()
    for copy in copies:
        copy.wait()
    total = None
    for v, first in ((va, first_a), (vb, leaves // 2 - first_a)):
        for pair in range(leaves // 4):
            leaf = first + 2 * pair
            rows = v[:, 2 * pair * points : 2 * (pair + 1) * points]
            both = paired_coef(rows, basis[leaf], basis[leaf + 1])
            at = columns_of((first // 2 + pair) * 2 * rank, 2 * rank)
            coef[:, at] = both
            term = mm(both, trans[at, :])
            total = term if total is None else total + term
    node[...] = total
    for copy in later:
        copy.wait()


def head(va, vb, basis_t, trans2, near_blocks):
    columns = va.shape[0]
    leaves, rank, _ = basis_t.shape
    arrays = (basis_t, trans2, near_blocks)
    hbm = (pltpu.with_memory_space_constraint(x, pltpu.HBM) for x in arrays)
    return pl.pallas_call(
        head_body,
        in_specs=[VMEM] * 2 + [HBM] * 3,
        out_specs=[VMEM] * 3,
        out_shape=[
            jax.ShapeDtypeStruct((columns, leaves * rank), BF),
            jax.ShapeDtypeStruct((columns, rank), F32),
            jax.ShapeDtypeStruct(near_blocks.shape, BF),
        ],
        scratch_shapes=[
            pltpu.VMEM(basis_t.shape, BF),
            pltpu.VMEM(trans2.shape, BF),
            pltpu.SemaphoreType.DMA((2 + leaves // PIECES,)),
        ],
        compiler_params=params(6),
        cost_estimate=cost(200_000_000, 6_000_000),
        name="head",
    )(va, vb, *hbm)


def table_body(
    levels, near_list, trans_hbm, couple_hbm, near, old_kept, up, pair, plan, kept, *scratch
):
    trans, couple, sems = scratch
    copies = [
        pltpu.make_async_copy(trans_hbm, trans, sems.at[0]),
        pltpu.make_async_copy(couple_hbm, couple, sems.at[1]),
    ]
    copies += load_piece(near, kept, 1, sems, 2)
    for copy in copies:
        copy.start()
    device = lax.axis_index("leaf")
    kn, leaves = near_list.shape
    first = device * leaves
    even = is_even()

    def scan(leaf, found):
        in_a, in_b = found
        for slot in range(kn):
            source = near_list[slot, leaf] - first
            left = source < 0
            outside = left | (source >= leaves)
            to_a = left != even
            code = (leaf * 8 + slot) * 16 + source + jnp.where(left, REACH, -leaves)
            plan[in_a] = code
            plan[LIST + in_b] = code
            in_a = in_a + jnp.where(outside & to_a, 1, 0)
            in_b = in_b + jnp.where(outside & jnp.logical_not(to_a), 1, 0)
        return in_a, in_b

    found = lax.fori_loop(0, leaves, scan, (jnp.int32(0), jnp.int32(0)))
    for side, total in enumerate(found):
        for i in range(TOGETHER):
            plan[side * LIST + total + i] = (leaves * 8) * 16
        plan[2 * LIST + side] = lax.div(total + TOGETHER - 1, TOGETHER)
    count, rows, nodes = 8, trans.shape[0], trans.shape[2]
    row = lax.broadcasted_iota(jnp.int32, (count, nodes), 0)
    node = lax.broadcasted_iota(jnp.int32, (count, nodes), 1)
    offset = (2 << levels) - lax.shift_right_logical(jnp.full_like(row, 2 << levels), row)
    here = offset + lax.shift_right_logical(jnp.zeros_like(row) + device, row)
    there = jnp.bitwise_xor(here, 1)
    wanted = row < levels
    pick_here = jnp.where(wanted & (node == here), 1.0, 0.0).astype(BF)
    pick_there = jnp.where(wanted & (node == there), 1.0, 0.0).astype(BF)
    both = jnp.concatenate([pick_here, pick_there], axis=0)
    copies[0].wait()
    copies[1].wait()
    for k in range(rows):
        picked = mm(both, trans[k], NT)
        up[0, :, k, :] = picked[:levels]
        up[1, :, k, :] = picked[count : count + levels]
        pair[:, k, :] = mm(pick_here, couple[k], NT)[:levels]
    for copy in copies[2:]:
        copy.wait()


def chain_body(up, pair, down):
    levels = pair.shape[0]
    down[0] = pair[0]
    path = up[0, 0]
    for t in range(1, levels):
        down[t] = exact(path, pair[t])
        if t + 1 < levels:
            path = exact(path, up[0, t])


def chain(up, pair):
    return pl.pallas_call(
        chain_body,
        in_specs=[VMEM] * 2,
        out_specs=VMEM,
        out_shape=jax.ShapeDtypeStruct(pair.shape, F32),
        compiler_params=params(4),
        cost_estimate=cost(10_000_000, 1_000_000),
        name="chain",
    )(up, pair)


def table(top_transfer, top_couple, near_list_t, near_blocks, kept):
    nodes, rank, _ = top_transfer.shape
    levels = lax.axis_size("leaf").bit_length() - 1
    shape = near_blocks.shape
    hbm = (
        jnp.transpose(top_transfer, (1, 2, 0)),
        jnp.transpose(top_couple, (1, 2, 0)),
        near_blocks,
    )
    return pl.pallas_call(
        lambda *refs: table_body(levels, *refs),
        grid_spec=pltpu.PrefetchScalarGridSpec(
            num_scalar_prefetch=1,
            in_specs=[HBM] * 3 + [VMEM],
            out_specs=[VMEM, VMEM, pl.BlockSpec(memory_space=pltpu.SMEM), VMEM],
            scratch_shapes=[
                pltpu.VMEM((rank, rank, nodes), BF),
                pltpu.VMEM((rank, rank, nodes), BF),
                pltpu.SemaphoreType.DMA((2 * (shape[0] // PIECES) + 2,)),
            ],
        ),
        out_shape=[
            jax.ShapeDtypeStruct((2, levels, rank, rank), F32),
            jax.ShapeDtypeStruct((levels, rank, rank), F32),
            jax.ShapeDtypeStruct((2 * LIST + 8,), jnp.int32),
            jax.ShapeDtypeStruct(shape, BF),
        ],
        input_output_aliases={4: 3},
        compiler_params=params(6),
        cost_estimate=cost(10_000_000, 8_000_000),
        name="table",
    )(near_list_t, *(pltpu.with_memory_space_constraint(x, pltpu.HBM) for x in hbm), kept)


def near_body(piece, load, near_list, v, kept, *refs):
    copies = []
    if load:
        near, total, kept, sems = refs
        copies = load_piece(near, kept, piece + 2, sems)
        for copy in copies:
            copy.start()
    else:
        (total,) = refs
    leaves, kn, points, _ = kept.shape
    some = leaves // PIECES
    first = lax.axis_index("leaf") * leaves
    for i in range(some):
        out = None
        leaf = piece * some + i
        for s in range(kn):
            source = near_list[s, leaf] - first
            inside = (source >= 0) & (source < leaves)
            rows = v[:, columns_of(jnp.clip(source, 0, leaves - 1) * points, points)]
            term = mm(jnp.where(inside, rows, jnp.zeros_like(rows)), kept[leaf, s], NT)
            out = term if out is None else out + term
        total[:, i * points : (i + 1) * points] = out
    for copy in copies:
        copy.wait()


def near_piece(piece, near_list_t, v, near_blocks, kept, load):
    columns = v.shape[0]
    leaves, _, points, _ = kept.shape
    some = leaves // PIECES
    in_specs = [VMEM, VMEM]
    args = [v, kept]
    out_shape = [jax.ShapeDtypeStruct((columns, some * points), F32)]
    scratch = []
    if load:
        in_specs.append(HBM)
        args.append(pltpu.with_memory_space_constraint(near_blocks, pltpu.HBM))
        out_shape.append(jax.ShapeDtypeStruct(kept.shape, BF))
        scratch.append(pltpu.SemaphoreType.DMA((some,)))
    return pl.pallas_call(
        lambda *refs: near_body(piece, load, *refs),
        grid_spec=pltpu.PrefetchScalarGridSpec(
            num_scalar_prefetch=1,
            in_specs=in_specs,
            out_specs=[VMEM] * len(out_shape),
            scratch_shapes=scratch,
        ),
        out_shape=out_shape,
        input_output_aliases={2: 1} if load else {},
        compiler_params=params(4),
        cost_estimate=cost(350_000_000, 6_000_000),
    )(near_list_t, *args)


def add_halo(side, plan, v, near, acc):
    leaves, _, points, _ = near.shape

    def add(j, carry):
        terms = []
        for i in range(TOGETHER):
            code = plan[side * LIST + j * TOGETHER + i]
            leaf = lax.shift_right_logical(code, 7)
            slot = lax.shift_right_logical(code, 4) & 7
            rows = v[:, columns_of((code & 15) * points, points)]
            term = mm(rows, near[leaf & (leaves - 1), slot], NT)
            terms.append((columns_of(leaf * points, points), term))
        for here, term in terms:
            acc[:, here] += term
        return carry

    lax.fori_loop(0, plan[2 * LIST + side], add, 0)


def unpack(coef, base, table_ref):
    wide = table_ref.shape[2]
    row = lax.broadcasted_iota(jnp.int32, (wide, wide), 0)
    lane = lax.broadcasted_iota(jnp.int32, (wide, wide), 1)
    swap = jnp.where(jnp.bitwise_xor(row, wide // 2) == lane, 1.0, 0.0).astype(BF)
    for pair in range(coef.shape[1] // wide):
        both = coef[:, wide * pair : wide * (pair + 1)]
        table_ref[base + 2 * pair] = both
        table_ref[base + 2 * pair + 1] = mm(both, swap).astype(BF)


def side_body(plan, got_va, got_ca, sent_c, near, *refs):
    partial, (acc, table_ref) = refs[:PIECES], refs[PIECES:]
    leaves = near.shape[0]
    for piece, part in enumerate(partial):
        width = part.shape[1]
        acc[:, piece * width : (piece + 1) * width] = part[...]
    unpack(sent_c, leaves, table_ref)
    unpack(got_ca, jnp.where(is_even(), 2 * leaves, 0), table_ref)
    add_halo(0, plan, got_va, near, acc)


def side_a(plan, got_va, got_ca, sent_c, kept, partial):
    columns = sent_c.shape[0]
    leaves, _, points, _ = kept.shape
    rank = sent_c.shape[1] // leaves
    return pl.pallas_call(
        side_body,
        grid_spec=pltpu.PrefetchScalarGridSpec(
            num_scalar_prefetch=1,
            in_specs=[VMEM] * (4 + PIECES),
            out_specs=[VMEM] * 2,
        ),
        out_shape=[
            jax.ShapeDtypeStruct((columns, (leaves + 1) * points), F32),
            jax.ShapeDtypeStruct((3 * leaves, columns, 2 * rank), BF),
        ],
        compiler_params=params(4),
        cost_estimate=cost(400_000_000, 6_000_000),
        name="side",
    )(plan, got_va, got_ca, sent_c, kept, *partial)


def side_b_body(plan, got_vb, got_cb, near, old_acc, old_table, acc, table_ref):
    leaves = near.shape[0]
    unpack(got_cb, jnp.where(is_even(), 0, 2 * leaves), table_ref)
    add_halo(1, plan, got_vb, near, acc)


def side_b(plan, got_vb, got_cb, kept, acc, entries):
    return pl.pallas_call(
        side_b_body,
        grid_spec=pltpu.PrefetchScalarGridSpec(
            num_scalar_prefetch=1,
            in_specs=[VMEM] * 5,
            out_specs=[VMEM] * 2,
        ),
        out_shape=[
            jax.ShapeDtypeStruct(acc.shape, acc.dtype),
            jax.ShapeDtypeStruct(entries.shape, entries.dtype),
        ],
        input_output_aliases={4: 0, 5: 1},
        compiler_params=params(4),
        cost_estimate=cost(200_000_000, 3_000_000),
        name="side_b",
    )(plan, got_vb, got_cb, kept, acc, entries)


def tail_body(names, sides, more, *refs):
    r = dict(zip(names, refs))
    acc, table_ref, couple_list = r["acc"], r["table"], r["couple_list"]
    basis, trans, couple, image = r["basis"], r["trans"], r["couple"], r["image"]
    leaves, rank, points = basis.shape
    group = leaves // 4
    even = is_even()
    first = lax.axis_index("leaf") * leaves
    first_b = jnp.where(even, 0, leaves // 2)
    descent = r["top"][...].astype(BF)
    own_v = r["own_v"]
    writes = []
    total = r["node_in"][...] if "node_in" in r else None
    for side in sides:
        start = first_b if side == "b" else leaves // 2 - first_b
        for part in range(2):
            base = start + part * group
            results = []
            for i in range(group):
                leaf = base + i
                moved = trans[columns_of(leaf * rank, rank), :]
                local = mm(descent, moved, NT)
                for s in range(couple.shape[1]):
                    source = couple_list[s, leaf] - first + FARR
                    local += mm(table_ref[source, :, :rank], couple[leaf, s], NT)
                here = columns_of(leaf * points, points)
                value = (acc[:, here] + mm(local.astype(BF), basis[leaf])).astype(BF)
                results.append(value)
                own_v[:, here] = value
                if more:
                    at = (part * group + i) * points
                    r["message"][:, at : at + points] = value
            here = columns_of(base * points, group * points)
            writes.append(
                pltpu.make_async_copy(own_v.at[:, here], image.at[:, here], r["sems"].at[len(writes)])
            )
            writes[-1].start()
            if not more:
                continue
            for pair in range(group // 2):
                leaf = base + 2 * pair
                rows = jnp.concatenate(results[2 * pair : 2 * pair + 2], axis=1)
                both = paired_coef(rows, basis[leaf], basis[leaf + 1])
                at = columns_of((base // 2 + pair) * 2 * rank, 2 * rank)
                r["coef"][:, at] = both
                term = mm(both, trans[at, :])
                total = term if total is None else total + term
    if more:
        r["node"][...] = total
    for write in writes:
        write.wait()


def tail(sides, more, scalars, inputs, carried):
    leaves, rank, points = inputs["basis"].shape
    columns = inputs["top"].shape[0]
    own = leaves * points
    fresh = {}
    if "image" not in carried:
        fresh["image"] = jax.ShapeDtypeStruct((columns, own), BF)
    if more:
        if "own_v" not in carried:
            fresh["own_v"] = jax.ShapeDtypeStruct((columns, own), BF)
            fresh["coef"] = jax.ShapeDtypeStruct((columns, leaves * rank), BF)
        fresh["message"] = jax.ShapeDtypeStruct((columns, own // 2), BF)
        fresh["node"] = jax.ShapeDtypeStruct((columns, rank), F32)
    outs = [*carried, *fresh]
    before = [*scalars, *inputs]
    names = [*before, *(f"old_{name}" for name in carried), *outs]
    scratch = [pltpu.SemaphoreType.DMA((4,))]
    names.append("sems")
    if not more:
        scratch.append(pltpu.VMEM((columns, own), BF))
        names.append("own_v")
    spec = lambda name: HBM if name == "image" else VMEM
    result = pl.pallas_call(
        lambda *refs: tail_body(names, sides, more, *refs),
        grid_spec=pltpu.PrefetchScalarGridSpec(
            num_scalar_prefetch=len(scalars),
            in_specs=[VMEM] * len(inputs) + [spec(name) for name in carried],
            out_specs=[spec(name) for name in outs],
            scratch_shapes=scratch,
        ),
        out_shape=[
            jax.ShapeDtypeStruct(carried[name].shape, carried[name].dtype)
            if name in carried
            else fresh[name]
            for name in outs
        ],
        input_output_aliases={len(before) + i: i for i in range(len(carried))},
        compiler_params=params(6),
        cost_estimate=cost(600_000_000, 6_000_000),
    )(*scalars.values(), *inputs.values(), *carried.values())
    return dict(zip(outs, result))


def swapped(value, mask):
    return lax.ppermute(value, "leaf", [(i, i ^ mask) for i in range(lax.axis_size("leaf"))])


def swapped_odd(value):
    size = lax.axis_size("leaf")
    pairs = [(i, i + 1) for i in range(1, size - 1, 2)]
    return lax.ppermute(value, "leaf", pairs + [(j, i) for i, j in pairs])


def one_product(node, va, coef, got_va, fill, tables):
    levels = lax.axis_size("leaf").bit_length() - 1
    top = jnp.zeros_like(node)
    got_ca = got_cb = None
    others = []
    for t in range(levels):
        mask = (1 << t) if t % 2 == 0 else 3 << (t - 1)
        other = swapped(node, mask)
        fill(t)
        up, down = tables(t)
        if t == 0:
            if got_va is None:
                got_va = swapped(va, 1)
            got_ca = swapped(coef, 1)
            got_cb = swapped_odd(coef)
        if t + 1 < levels:
            node = exact(node, up[0, t]) + exact(other, up[1, t])
        others.append(other)
    for t, other in enumerate(others):
        top += exact(other, down[t], NT)
    return top, got_va, got_ca, got_cb


def on_device(
    rhs_block,
    basis_t,
    near_blocks,
    near_list,
    leaf_transfer,
    couple_list,
    leaf_couple,
    top_transfer,
    top_couple,
):
    leaves, rank, _ = leaf_transfer.shape
    trans2 = leaf_transfer.reshape(leaves * rank, rank)
    near_list_t, couple_list_t = near_list.T, couple_list.T
    made = {}
    partial, again = [], []

    def fill_first(t):
        if t == 0:
            made["up"], made["pair"], made["plan"], made["kept"] = table(
                top_transfer, top_couple, near_list_t, near_blocks, made["kept"]
            )
        elif t <= PIECES:
            load = t + 1 < PIECES
            out = near_piece(t - 1, near_list_t, rhs_block, near_blocks, made["kept"], load)
            partial.append(out[0])
            if load:
                made["kept"] = out[1]

    def tables(t):
        if t == 4 and "down" not in made:
            made["down"] = chain(made["up"], made["pair"])
        return made["up"], made.get("down")

    def fill_second(t):
        for piece in {1: (0, 1), 2: (2,), 3: (3,)}.get(t, ()):
            (out,) = near_piece(piece, near_list_t, made["own_v"], near_blocks, made["kept"], False)
            again.append(out)

    scalars = {"couple_list": couple_list_t}

    def parts(top):
        return {"top": top, "basis": basis_t, "trans": trans2, "couple": leaf_couple}

    def sides(got_va, got_vb, got_ca, got_cb, coef, own):
        acc, entries = side_a(made["plan"], got_va, got_ca, coef, made["kept"], own)
        acc, entries = side_b(made["plan"], got_vb, got_cb, made["kept"], acc, entries)
        return {"acc": acc, "table": entries}

    va, vb = split(rhs_block)
    got_va = swapped(va, 1)
    got_vb = swapped_odd(vb)
    coef, node, made["kept"] = head(va, vb, basis_t, trans2, near_blocks)
    top, _, got_ca, got_cb = one_product(node, va, coef, got_va, fill_first, tables)
    carried = sides(got_va, got_vb, got_ca, got_cb, coef, partial)
    inputs = parts(top)
    half = tail("b", True, scalars, inputs, carried)
    got_vb = swapped_odd(half["message"])
    inputs = {**inputs, "node_in": half["node"]}
    carried = {k: half[k] for k in ("acc", "table", "image", "own_v", "coef")}
    rest = tail("a", True, scalars, inputs, carried)
    first_image, coef, made["own_v"] = rest["image"], rest["coef"], rest["own_v"]
    top, got_va, got_ca, got_cb = one_product(
        rest["node"], rest["message"], coef, None, fill_second, tables
    )
    carried = sides(got_va, got_vb, got_ca, got_cb, coef, again)
    last = tail("ba", False, scalars, parts(top), carried)
    return (first_image, last["image"])


def solution(mesh):
    in_specs = (
        P("rhs", "leaf"),
        P("leaf", None, None),
        P("leaf", None, None, None),
        P("leaf", None),
        P("leaf", None, None),
        P("leaf", None),
        P("leaf", None, None, None),
        P(),
        P(),
    )
    out_specs = (P("rhs", "leaf"), P("rhs", "leaf"))
    return jax.shard_map(
        on_device, mesh=mesh, in_specs=in_specs, out_specs=out_specs, check_vma=False
    )
```
